256 devices in a mesh: gx: 32 (over y, z_lo, x), gy: 8 (over z_hi, core).
Axes of the slice: x: 4, y: 4, z: 8 (z_hi: 4, z_lo: 2; z = z_hi * 2 + z_lo), core: 2. Of those that a mesh axis runs over, the one named last changes fastest.
Arguments:
- residual: bfloat16 [32, 8, 2048, 384], P('gx', 'gy'), may hold values from -6 to 6
- local_inverse: bfloat16 [32, 8, 2048, 2048], P('gx', 'gy'), may hold values from -0.125 to 0.125
- primal_basis: bfloat16 [32, 8, 96, 2048], P('gx', 'gy'), may hold values from -0.125 to 0.125
- row_stiffness: bfloat16 [32, 8, 2048], P('gx', 'gy'), may hold values from 0.099609375 to 10
- face_sizes: int32 [32, 8, 4], P('gx', 'gy'), may hold values from 0 to 512, as said below
- primal_slots: int32 [32, 8, 96], P('gx', 'gy'), may hold values from 0 to 287
- block_inverse: float32 [32, 8, 32, 256], P('gx', 'gy'), may hold values from -1 to 3
- level_basis: float32 [32, 8, 32, 64], P('gx', 'gy'), may hold values from -0.15625 to 0.15625
- top_inverse: float32 [64, 64], replicated, may hold values from -1 to 3
Outputs:
- preconditioned: bfloat16 [32, 8, 2048, 384], P('gx', 'gy')
The draws below stay inside these ranges and needn't reach their ends.
Inputs may be any that keep to these rules, and one draw needn't show every extreme that they name: face_sizes[x, y, f] is equal on the two sides of a shared face, 0 on faces at the grid's edge, at least 128 elsewhere; the value 512 is reached.
All inputs are finite; a program needn't handle non-finite values.
Results may differ from the reference program's by a relative error of at most 0.008.
Values may be sent and summed in bfloat16 or wider, within the bound.
A program may use at most 64 MiB of HBM per device.

```python
import math
import jax
import jax.numpy as jnp
from jax import lax

W = 2048
R = 384
P_SIZE = 96
CDEV = 32
L3 = 64
SUBX = 32
SUBY = 8
CBS = 256


def draw_face_sizes(key, part):
    face_rows = W // 4
    key_x = jax.random.fold_in(key, 11)
    key_y = jax.random.fold_in(key, 12)
    edges_x = jax.random.randint(key_x, (SUBX - 1, SUBY), face_rows // 4, face_rows + 1, dtype=jnp.int32)
    edges_x = edges_x.at[0, 0].set(face_rows)
    edges_y = jax.random.randint(key_y, (SUBX, SUBY - 1), face_rows // 4, face_rows + 1, dtype=jnp.int32)
    blank_x = jnp.zeros((1, SUBY), jnp.int32)
    blank_y = jnp.zeros((SUBX, 1), jnp.int32)
    lower_x = jnp.concatenate([blank_x, edges_x], axis=0)
    upper_x = jnp.concatenate([edges_x, blank_x], axis=0)
    lower_y = jnp.concatenate([blank_y, edges_y], axis=1)
    upper_y = jnp.concatenate([edges_y, blank_y], axis=1)
    return jnp.stack([lower_x, upper_x, lower_y, upper_y], axis=-1)


def noise_field(key, shape):
    return jnp.clip(jax.random.normal(key, shape, jnp.float32), -4.0, 4.0)


def draw_block_inverse(key, part):
    key_noise = jax.random.fold_in(key, 21)
    key_diag = jax.random.fold_in(key, 22)
    noise = noise_field(key_noise, (SUBX, SUBY, CDEV, CBS))
    diagonal = jnp.exp(jax.random.uniform(key_diag, (SUBX, SUBY, CDEV, 1), jnp.float32, -0.7, 0.7))
    target = jnp.arange(SUBY)[:, None] * CDEV + jnp.arange(CDEV)[None, :]
    on_diag = jnp.arange(CBS)[None, None, :] == target[:, :, None]
    return 0.5 * noise / math.sqrt(CBS) + jnp.where(on_diag[None], diagonal, 0.0)


def draw_top_inverse(key, part):
    key_noise = jax.random.fold_in(key, 31)
    key_diag = jax.random.fold_in(key, 32)
    noise = noise_field(key_noise, (L3, L3))
    diagonal = jnp.exp(jax.random.uniform(key_diag, (L3, 1), jnp.float32, -0.7, 0.7))
    on_diag = jnp.arange(L3)[:, None] == jnp.arange(L3)[None, :]
    return 0.5 * noise / math.sqrt(L3) + jnp.where(on_diag, diagonal, 0.0)


def with_ends(result, own_key, low, largest):
    longest = result.shape.index(max(result.shape))
    spots = []
    for shift in (0, 1):
        where = [jax.random.randint(jax.random.fold_in(own_key, axis), (), 0, length) for axis, length in enumerate(result.shape)]
        where[longest] = (where[longest] + shift) % result.shape[longest]
        spots.append(tuple(where))
    return result.at[spots[0]].set(low).at[spots[1]].set(largest)


def levels(own_key, shape, shards, least, high):
    def one(dim, blocks):
        draws = jax.random.uniform(jax.random.fold_in(jax.random.fold_in(own_key, 6), dim), (blocks,), jnp.float32, least / len(shards), high / len(shards))
        return jnp.repeat(jnp.exp(draws), shape[dim] // blocks).reshape((-1,) + (1,) * (len(shape) - dim - 1))

    loudness = one(*shards[0])
    for cut in shards[1:]:
        loudness = loudness * one(*cut)
    return loudness


def gaussian(key, dims, width, most, shards=(), kind=jnp.bfloat16):
    result = jax.random.normal(key, dims, jnp.float32) * width
    if len(shards) > 0:
        result = levels(key, dims, shards, -0.22, 0.18) * result
    return jnp.clip(result, min=-most, max=most).astype(kind)


def setup_inputs(seed: int = 0) -> dict:
    streams_of = jax.random.split(jax.random.key(seed), 10)
    residual = gaussian(streams_of[0], (SUBX, SUBY, W, R), 1.0, 6.0, ((0, 32), (1, 8)))
    local_inverse = gaussian(streams_of[1], (SUBX, SUBY, W, W), W ** -0.5, 0.125, ((0, 32), (1, 8)))
    primal_basis = gaussian(streams_of[2], (SUBX, SUBY, P_SIZE, W), W ** -0.5, 0.125, ((0, 32), (1, 8)))
    row_stiffness = jnp.clip(jnp.exp(math.log(10.0) - 4.609084 * jax.random.uniform(streams_of[3], (SUBX, SUBY, W), jnp.float32) ** levels(streams_of[3], (SUBX, SUBY, W), ((0, 32), (1, 8)), -0.2, 0.2)), 0.099609375, 10.0).astype(jnp.bfloat16)
    face_sizes = draw_face_sizes(jax.random.fold_in(streams_of[9], 71), 0)
    primal_slots = with_ends(jax.random.randint(streams_of[5], (SUBX, SUBY, P_SIZE), 0, 9 * CDEV), jax.random.fold_in(streams_of[5], 1), 0, (9 * CDEV) - 1).astype(jnp.int32)
    block_inverse = draw_block_inverse(jax.random.fold_in(streams_of[9], 71), 0)
    level_basis = gaussian(streams_of[7], (SUBX, SUBY, CDEV, L3), (48 * CDEV) ** -0.5, 0.15625, ((0, 32), (1, 8)), jnp.float32)
    top_inverse = draw_top_inverse(jax.random.fold_in(streams_of[9], 71), 0)
    return dict(residual=residual, local_inverse=local_inverse, primal_basis=primal_basis, row_stiffness=row_stiffness, face_sizes=face_sizes, primal_slots=primal_slots, block_inverse=block_inverse, level_basis=level_basis, top_inverse=top_inverse)


def partner_rows(values):
    face_rows = W // 4
    tail = values.shape[3:]
    parts = values.reshape((SUBX, SUBY, 4, face_rows) + tail)
    rest = [(0, 0)] * (len(tail) + 1)
    low_x = jnp.pad(parts[:, :, 1], [(1, 0), (0, 0)] + rest)[:SUBX]
    high_x = jnp.pad(parts[:, :, 0], [(0, 1), (0, 0)] + rest)[1:]
    low_y = jnp.pad(parts[:, :, 3], [(0, 0), (1, 0)] + rest)[:, :SUBY]
    high_y = jnp.pad(parts[:, :, 2], [(0, 0), (0, 1)] + rest)[:, 1:]
    return jnp.stack([low_x, high_x, low_y, high_y], axis=2).reshape(values.shape)


def reference(residual, local_inverse, primal_basis, row_stiffness, face_sizes, primal_slots, block_inverse, level_basis, top_inverse):
    highest = lax.Precision.HIGHEST
    face_rows = W // 4
    position = jnp.arange(W, dtype=jnp.int32)
    face_of_row = position // face_rows
    counts = face_sizes[:, :, face_of_row]
    live_rows = (position % face_rows)[None, None, :] < counts
    masked = jnp.where(live_rows[..., None], residual, jnp.zeros((), jnp.bfloat16))

    def local_solve(subdomain):
        inverse, own_rows, primal_phi = subdomain
        return (jnp.dot(inverse, own_rows, preferred_element_type=jnp.float32),
                jnp.dot(primal_phi, own_rows, preferred_element_type=jnp.float32))

    local_part, partial_value = lax.map(local_solve, (local_inverse.reshape(SUBX * SUBY, W, W),
                                                masked.reshape(SUBX * SUBY, W, R),
                                                primal_basis.reshape(SUBX * SUBY, P_SIZE, W)))
    local_part = local_part.reshape(SUBX, SUBY, W, R)
    partial_value = partial_value.reshape(SUBX, SUBY, P_SIZE, R)
    selector = (primal_slots[..., None] == jnp.arange(9 * CDEV, dtype=jnp.int32)).astype(jnp.float32)
    spread = jnp.einsum('xyps,xypr->xysr', selector, partial_value, precision=highest).reshape(SUBX, SUBY, 3, 3, CDEV, R)
    padded = jnp.pad(spread, ((1, 1), (1, 1), (0, 0), (0, 0), (0, 0), (0, 0)))
    assembled = jnp.zeros((SUBX, SUBY, CDEV, R), jnp.float32)
    for shift_x in range(3):
        for shift_y in range(3):
            assembled = assembled + padded[2 - shift_x:2 - shift_x + SUBX, 2 - shift_y:2 - shift_y + SUBY, shift_x, shift_y]
    block_rhs = assembled.reshape(SUBX, SUBY * CDEV, R)
    top_rhs = jnp.einsum('xycl,xycr->lr', level_basis, assembled, precision=highest)
    top_value = jnp.dot(top_inverse, top_rhs, precision=highest)
    coarse = jnp.einsum('xycs,xsr->xycr', block_inverse, block_rhs, precision=highest)
    coarse = coarse + jnp.einsum('xycl,lr->xycr', level_basis, top_value, precision=highest)
    coarse_pad = jnp.pad(coarse, ((1, 1), (1, 1), (0, 0), (0, 0)))
    beside_all = jnp.stack([coarse_pad[shift_x:shift_x + SUBX, shift_y:shift_y + SUBY]
                        for shift_x in range(3) for shift_y in range(3)], axis=2).reshape(SUBX, SUBY, 9 * CDEV, R)
    primal_values = jnp.einsum('xyps,xysr->xypr', selector, beside_all, precision=highest)
    stiffness = row_stiffness.astype(jnp.float32)
    coarse_rows = jnp.einsum('xypw,xypr->xywr', primal_basis.astype(jnp.float32), primal_values, precision=highest)
    sent = jnp.where(live_rows[..., None], stiffness[..., None] * local_part + stiffness[..., None] * coarse_rows, 0.0).astype(jnp.bfloat16)
    summed = sent.astype(jnp.float32) + partner_rows(sent).astype(jnp.float32)
    divisor = stiffness + partner_rows(row_stiffness).astype(jnp.float32)
    return jnp.where(live_rows[..., None], summed / divisor[..., None], 0.0).astype(jnp.bfloat16)
```

```python
import functools

import jax
import jax.numpy as jnp
from jax import lax
from jax.experimental import pallas as pl
from jax.experimental.pallas import tpu as pltpu
from jax.sharding import PartitionSpec as P

MESH = pl.DeviceIdType.MESH
HIGHEST = lax.Precision.HIGHEST
F32 = jnp.float32
BF16 = jnp.bfloat16
RUN = 4
OFFSETS = [(a, b) for a in (-1, 0, 1) for b in (-1, 0, 1) if (a, b) != (0, 0)]
FACES = [(-1, 0), (1, 0), (0, -1), (0, 1)]
TILE = 256


def dot(a, b, dims=((1,), (0,)), precision=None):
    return lax.dot_general(a, b, (dims, ((), ())), preferred_element_type=F32, precision=precision)


def slot_of(a, b):
    return (a + 1) * 3 + (b + 1)


def apply_kernel(
    gx_count,
    gy_count,
    res_h, inv_h, phi_h, stiff_h, sizes_h, slots_h, block_h, level_h, topinv_h,
    acc_h, w_h, top_h,
    res, inv, phi, stiff, sizes, slots, block, level, topinv,
    masked, col, dencol, lev_ext, partial, part_send, part_recv, asm, blk, coarse_ext,
    stat_send, stat_recv, bulk_send, bulk_recv, low_send, low_recv,
    red_send, red_recv, run_send, run_recv, far_send, far_recv, piece_send, top,
    acc, wt,
    load_sem, inv_sem, out_sem,
    lev_s, lev_r, part_s, part_r, coarse_s, coarse_r,
    stat_s, stat_r, bulk_s, bulk_r, low_s, low_r,
    red_s, red_r, asm_s, asm_r, run_s, run_r, far_s, far_r, top_s, top_r,
):
    x = lax.axis_index("gx")
    y = lax.axis_index("gy")
    rows, width = res.shape
    face = rows // 4
    primal = phi.shape[0]
    cdev, top_size = level.shape
    far_count = gx_count // RUN
    piece = top_size // gy_count
    pending = []

    def inside(a, b):
        ok_x = jnp.logical_and(x + a >= 0, x + a < gx_count)
        ok_y = jnp.logical_and(y + b >= 0, y + b < gy_count)
        return jnp.logical_and(ok_x, ok_y)

    def remote(src, dst, send, recv, dev):
        return pltpu.make_async_remote_copy(
            src_ref=src, dst_ref=dst, send_sem=send, recv_sem=recv,
            device_id=dev, device_id_type=MESH)

    def beside(a, b, src, dst, send, recv):
        @pl.when(inside(a, b))
        def _():
            remote(src, dst, send, recv, (x + a, y + b)).start()

        def done():
            @pl.when(inside(a, b))
            def _():
                remote(src, dst, send, recv, (x + a, y + b)).wait_send()
        pending.append(done)

    def arrived(a, b, dst, send, recv):
        @pl.when(inside(a, b))
        def _():
            remote(dst, dst, send, recv, (x + a, y + b)).wait_recv()

    def zero_outside(a, b, ref):
        @pl.when(jnp.logical_not(inside(a, b)))
        def _():
            ref[...] = jnp.zeros(ref.shape, ref.dtype)

    def gy_peer(d):
        return (x, lax.rem(y + d, gy_count))

    def run_peer(d):
        return (x - lax.rem(x, RUN) + lax.rem(lax.rem(x, RUN) + d, RUN), y)

    def far_peer(d):
        return (lax.rem(x // RUN + d, far_count) * RUN + lax.rem(x, RUN), y)

    def to_group(peer, d, src, dst, send, recv):
        remote(src, dst, send.at[d], recv.at[d], peer(d)).start()
        pending.append(lambda: remote(src, dst, send.at[d], recv.at[d], peer(d)).wait_send())

    def group_arrived(peer, d, dst, send, recv):
        remote(dst, dst, send.at[d], recv.at[d], peer(d)).wait_recv()

    loads = [
        pltpu.make_async_copy(src, dst, load_sem.at[i])
        for i, (src, dst) in enumerate([
            (level_h, level), (slots_h, slots), (sizes_h, sizes), (stiff_h, stiff),
            (topinv_h, topinv), (block_h, block), (phi_h, phi)])
    ]
    res_loads = [
        pltpu.make_async_copy(
            res_h.at[pl.ds(f * face, face)], res.at[pl.ds(f * face, face)],
            load_sem.at[len(loads) + f])
        for f in range(4)
    ]
    inv_loads = [
        pltpu.make_async_copy(
            inv_h.at[pl.ds(f * face, face)], inv.at[pl.ds(f * face, face)], inv_sem.at[f])
        for f in range(4)
    ]
    for copy in loads + res_loads + inv_loads:
        copy.start()
    barrier = pltpu.get_barrier_semaphore()
    for a, b in OFFSETS:
        @pl.when(inside(a, b))
        def _():
            pl.semaphore_signal(barrier, inc=1, device_id=(x + a, y + b), device_id_type=MESH)
    for peer, count in ((gy_peer, gy_count), (run_peer, RUN), (far_peer, far_count)):
        for d in range(1, count):
            pl.semaphore_signal(barrier, inc=1, device_id=peer(d), device_id_type=MESH)

    for a, b in OFFSETS:
        zero_outside(a, b, lev_ext.at[slot_of(a, b)])
        zero_outside(a, b, part_recv.at[slot_of(a, b)])
        zero_outside(a, b, coarse_ext.at[slot_of(a, b)])
    for f, (a, b) in enumerate(FACES):
        zero_outside(a, b, stat_recv.at[f])
        zero_outside(a, b, bulk_recv.at[f])
        zero_outside(a, b, low_recv.at[f])

    for copy in loads:
        copy.wait()
    slot_row = jnp.broadcast_to(slots[...], (9 * cdev, primal))
    slot_iota = lax.broadcasted_iota(jnp.int32, (9 * cdev, primal), 0)
    sel_t = jnp.where(slot_row == slot_iota, 1.0, 0.0).astype(F32)
    sel_t16 = sel_t.astype(BF16)
    lev_ext[slot_of(0, 0)] = level[...]

    def one(flag):
        return jnp.where(flag, 1, 0)

    count_x = 1 + one(x > 0) + one(x < gx_count - 1)
    count_y = 1 + one(y > 0) + one(y < gy_count - 1)
    pl.semaphore_wait(
        barrier, count_x * count_y - 1 + gy_count - 1 + RUN - 1 + far_count - 1)

    for i, (a, b) in enumerate(OFFSETS):
        beside(a, b, level, lev_ext.at[slot_of(-a, -b)], lev_s.at[i], lev_r.at[slot_of(-a, -b)])

    for f in range(4):
        res_loads[f].wait()
        live = lax.broadcasted_iota(jnp.int32, (face, width), 0) < sizes[0, f]
        part = res[pl.ds(f * face, face), :].astype(F32)
        masked[pl.ds(f * face, face), :] = jnp.where(live, part, 0.0).astype(BF16)
    partial[...] = dot(phi[...], masked[...])
    spread = dot(sel_t16, partial[...].astype(BF16))
    for k in range(9):
        part_send[k] = spread[k * cdev:(k + 1) * cdev].astype(BF16)
    for i, (a, b) in enumerate(OFFSETS):
        beside(a, b, part_send.at[slot_of(a, b)], part_recv.at[slot_of(-a, -b)],
               part_s.at[i], part_r.at[slot_of(-a, -b)])

    stiff32 = stiff[...].astype(F32)
    for f, (a, b) in enumerate(FACES):
        stat_send[f, :primal, :] = phi[:, f * face:(f + 1) * face]
        stat_send[f, primal:, :] = jnp.broadcast_to(
            stiff32[:, f * face:(f + 1) * face], (16, face)).astype(BF16)
        beside(a, b, stat_send.at[f], stat_recv.at[f ^ 1], stat_s.at[f], stat_r.at[f ^ 1])

    for a, b in OFFSETS:
        arrived(a, b, lev_ext.at[slot_of(a, b)], lev_s.at[0], lev_r.at[slot_of(a, b)])
    lev_all = lev_ext[...].reshape(9 * cdev, top_size)
    basis = dot(sel_t, lev_all, ((0,), (0,)), HIGHEST)
    basis_inv = dot(basis, topinv[...], ((1,), (1,)), HIGHEST)
    red_send[...] = dot(basis_inv, partial[...], ((0,), (0,)), HIGHEST)

    def piece_rows(index):
        return pl.ds(pl.multiple_of(index * piece, piece), piece)

    for d in range(1, gy_count):
        to_group(gy_peer, d, red_send.at[piece_rows(lax.rem(y + d, gy_count))],
                 red_recv.at[d], red_s, red_r)

    total = part_send[slot_of(0, 0)].astype(F32)
    for a, b in OFFSETS:
        arrived(a, b, part_recv.at[slot_of(a, b)], part_s.at[0], part_r.at[slot_of(a, b)])
        total = total + part_recv[slot_of(a, b)].astype(F32)
    asm[...] = total.astype(BF16)
    own_rows = pl.ds(pl.multiple_of(y * cdev, cdev), cdev)
    for d in range(1, gy_count):
        to_group(gy_peer, d, asm, blk.at[own_rows], asm_s, asm_r)
    blk[own_rows, :] = total.astype(BF16)

    for f in range(4):
        lane = lax.broadcasted_iota(jnp.int32, (1, face), 1)
        weight = jnp.where(lane < sizes[0, f], stiff32[:, f * face:(f + 1) * face], 0.0)
        for j in range(face // 128):
            square = jnp.broadcast_to(weight[:, j * 128:(j + 1) * 128], (128, 128))
            col[pl.ds(f * face + j * 128, 128), :] = square.T

    tile = min(TILE, face)

    def across(column):
        return jnp.concatenate([column] * (width // 128), axis=1)

    def local_face(f):
        inv_loads[f].wait()

        def step(i, carry):
            first = pl.multiple_of(f * face + i * tile, tile)
            value = dot(inv[pl.ds(first, tile), :], masked[...])
            value = value * across(col[pl.ds(first, tile), :])
            bulk_send[f, pl.ds(pl.multiple_of(i * tile, tile), tile), :] = value.astype(BF16)
            return carry

        lax.fori_loop(0, face // tile, step, 0)
        a, b = FACES[f]
        beside(a, b, bulk_send.at[f], bulk_recv.at[f ^ 1], bulk_s.at[f], bulk_r.at[f ^ 1])

    local_face(0)
    local_face(1)

    total = red_send[piece_rows(y), :]
    for d in range(1, gy_count):
        group_arrived(gy_peer, d, red_recv.at[d], red_s, red_r)
        total = total + red_recv[d]
    run_send[...] = total
    for d in range(1, RUN):
        to_group(run_peer, d, run_send, run_recv.at[d], run_s, run_r)
    local_face(2)
    total = run_send[...]
    for d in range(1, RUN):
        group_arrived(run_peer, d, run_recv.at[d], run_s, run_r)
        total = total + run_recv[d]
    far_send[...] = total
    for d in range(1, far_count):
        to_group(far_peer, d, far_send, far_recv.at[d], far_s, far_r)

    for d in range(1, gy_count):
        group_arrived(gy_peer, d, asm, asm_s, asm_r)
    coarse = dot(block[...], blk[...].astype(F32), precision=HIGHEST)
    coarse_ext[slot_of(0, 0)] = coarse.astype(BF16)
    for i, (a, b) in enumerate(OFFSETS):
        beside(a, b, coarse_ext.at[slot_of(0, 0)], coarse_ext.at[slot_of(-a, -b)],
               coarse_s.at[i], coarse_r.at[slot_of(-a, -b)])
    local_face(3)

    total = far_send[...]
    for d in range(1, far_count):
        group_arrived(far_peer, d, far_recv.at[d], far_s, far_r)
        total = total + far_recv[d]
    piece_send[...] = total
    for d in range(1, gy_count):
        to_group(gy_peer, d, piece_send, top.at[piece_rows(y)], top_s, top_r)
    top[piece_rows(y), :] = total

    for a, b in OFFSETS:
        arrived(a, b, coarse_ext.at[slot_of(a, b)], coarse_s.at[0], coarse_r.at[slot_of(a, b)])
    ext = coarse_ext[...].reshape(9 * cdev, width)
    low_send[:, :width] = dot(sel_t16, ext, ((0,), (0,))).astype(BF16)
    low_send[:, width:] = jnp.concatenate(
        [basis, jnp.zeros((primal, low_send.shape[1] - width - top_size), F32)], axis=1
    ).astype(BF16)
    for f, (a, b) in enumerate(FACES):
        beside(a, b, low_send, low_recv.at[f ^ 1], low_s.at[f], low_r.at[f ^ 1])

    outs = []
    for f, (a, b) in enumerate(FACES):
        arrived(a, b, stat_recv.at[f], stat_s.at[f], stat_r.at[f])
        lane = lax.broadcasted_iota(jnp.int32, (1, face), 1)
        live = lane < sizes[0, f]
        own = stiff32[:, f * face:(f + 1) * face]
        other = stat_recv[f, primal:primal + 8, :].astype(F32)[:1]
        scale = jnp.where(live, 1.0 / (own + other), 0.0)
        for j in range(face // 128):
            square = jnp.broadcast_to(scale[:, j * 128:(j + 1) * 128], (128, 128))
            dencol[pl.ds(f * face + j * 128, 128), :] = square.T
        own_phi = (stat_send[f, :primal, :].astype(F32) * (own * scale)).astype(BF16)
        other_phi = (stat_recv[f, :primal, :].astype(F32) * (other * scale)).astype(BF16)
        arrived(a, b, low_recv.at[f], low_s.at[f], low_r.at[f])
        both = dot(own_phi, low_send[...], ((0,), (0,))) + dot(other_phi, low_recv[f], ((0,), (0,)))
        arrived(a, b, bulk_recv.at[f], bulk_s.at[f], bulk_r.at[f])
        here = pl.ds(f * face, face)
        summed = bulk_send[f].astype(F32) + bulk_recv[f].astype(F32)
        acc[here, :] = both[:, :width] + summed * across(dencol[here, :])
        wt[here, :] = both[:, width:].astype(BF16)
        for k, (src, dst) in enumerate(((acc, acc_h), (wt, w_h))):
            copy = pltpu.make_async_copy(src.at[here], dst.at[here], out_sem.at[2 * f + k])
            copy.start()
            outs.append(copy)

    for d in range(1, gy_count):
        group_arrived(gy_peer, d, top.at[piece_rows(0)], top_s, top_r)
    copy = pltpu.make_async_copy(top, top_h, out_sem.at[8])
    copy.start()
    outs.append(copy)
    for copy in outs:
        copy.wait()
    for done in pending:
        done()


def finish_kernel(acc, wt, top, out):
    value = dot(wt[:, :top.shape[0]], top[...].astype(BF16))
    out[...] = (acc[...] + value).astype(BF16)


def local(gx_count, gy_count, residual, local_inverse, primal_basis, row_stiffness,
          face_sizes, primal_slots, block_inverse, level_basis, top_inverse):
    rows, width = residual.shape[2:]
    face = rows // 4
    primal = primal_basis.shape[2]
    cdev, top_size = level_basis.shape[2:]
    block_size = block_inverse.shape[3]
    far_count = gx_count // RUN
    piece = top_size // gy_count
    low_width = width + 128
    vm = pltpu.VMEM
    dma = pltpu.SemaphoreType.DMA
    args = (residual[0, 0], local_inverse[0, 0], primal_basis[0, 0], row_stiffness[0],
            face_sizes[0], primal_slots[0], block_inverse[0, 0], level_basis[0, 0], top_inverse)
    halo = dma((9,))
    four = dma((4,))
    gys = dma((gy_count,))
    scratch = [
        vm((rows, width), BF16), vm((rows, rows), BF16), vm((primal, rows), BF16),
        vm((1, rows), BF16), pltpu.SMEM((1, 4), jnp.int32), vm((1, primal), jnp.int32),
        vm((cdev, block_size), F32), vm((cdev, top_size), F32), vm((top_size, top_size), F32),
        vm((rows, width), BF16), vm((rows, 128), F32), vm((rows, 128), F32),
        vm((9, cdev, top_size), F32), vm((primal, width), F32),
        vm((9, cdev, width), BF16), vm((9, cdev, width), BF16),
        vm((cdev, width), BF16), vm((block_size, width), BF16), vm((9, cdev, width), BF16),
        vm((4, primal + 16, face), BF16), vm((4, primal + 16, face), BF16),
        vm((4, face, width), BF16), vm((4, face, width), BF16),
        vm((primal, low_width), BF16), vm((4, primal, low_width), BF16),
        vm((top_size, width), F32), vm((gy_count, piece, width), F32),
        vm((piece, width), F32), vm((RUN, piece, width), F32),
        vm((piece, width), F32), vm((far_count, piece, width), F32),
        vm((piece, width), F32), vm((top_size, width), F32),
        vm((rows, width), F32), vm((rows, 128), BF16),
        dma((11,)), four, dma((9,)),
        halo, halo, halo, halo, halo, halo,
        four, four, four, four, four, four,
        gys, gys, gys, gys, dma((RUN,)), dma((RUN,)), dma((far_count,)), dma((far_count,)),
        gys, gys,
    ]
    acc, wt, top = pl.pallas_call(
        functools.partial(apply_kernel, gx_count, gy_count),
        name="apply",
        out_shape=(
            jax.ShapeDtypeStruct((rows, width), F32),
            jax.ShapeDtypeStruct((rows, 128), BF16),
            jax.ShapeDtypeStruct((top_size, width), F32),
        ),
        in_specs=[pl.BlockSpec(memory_space=pl.ANY)] * len(args),
        out_specs=[pl.BlockSpec(memory_space=pl.ANY)] * 3,
        scratch_shapes=scratch,
        compiler_params=pltpu.CompilerParams(
            collective_id=0, has_side_effects=True, vmem_limit_bytes=56 << 20),
    )(*args)
    out = pl.pallas_call(
        finish_kernel,
        name="finish",
        grid=(4,),
        out_shape=jax.ShapeDtypeStruct((rows, width), BF16),
        in_specs=[
            pl.BlockSpec((face, width), lambda i: (i, 0)),
            pl.BlockSpec((face, 128), lambda i: (i, 0)),
            pl.BlockSpec((top_size, width), lambda i: (0, 0)),
        ],
        out_specs=pl.BlockSpec((face, width), lambda i: (i, 0)),
    )(acc, wt, top)
    return out[None, None]


def solution(mesh):
    in_specs = (
        P("gx", "gy", None, None),
        P("gx", "gy", None, None),
        P("gx", "gy", None, None),
        P("gx", "gy", None),
        P("gx", "gy", None),
        P("gx", "gy", None),
        P("gx", "gy", None, None),
        P("gx", "gy", None, None),
        P(),
    )
    out_specs = P("gx", "gy", None, None)
    body = functools.partial(local, mesh.shape["gx"], mesh.shape["gy"])
    return jax.shard_map(body, mesh=mesh, in_specs=in_specs, out_specs=out_specs, check_vma=False)
```

```python
import functools

import jax
import jax.numpy as jnp
from jax import lax
from jax.experimental import pallas as pl
from jax.experimental.pallas import tpu as pltpu
from jax.sharding import PartitionSpec as P

MESH = pl.DeviceIdType.MESH
HIGHEST = lax.Precision.HIGHEST
F32 = jnp.float32
BF16 = jnp.bfloat16
RUN = 4
OFFSETS = [(a, b) for a in (-1, 0, 1) for b in (-1, 0, 1) if (a, b) != (0, 0)]
FACES = [(-1, 0), (1, 0), (0, -1), (0, 1)]


def dot(a, b, dims=((1,), (0,)), precision=None):
    return lax.dot_general(a, b, (dims, ((), ())), preferred_element_type=F32, precision=precision)


def slot_of(a, b):
    return (a + 1) * 3 + (b + 1)


def apply_kernel(
    gx_count,
    gy_count,
    res_h, inv_h, phi_h, stiff_h, sizes_h, slots_h, block_h, level_h, topinv_h,
    acc, phit, low_out, lowr_out, top_out,
    res, inv, phi, stiff, sizes, slots, block, level, topinv,
    masked, col, dencol, lev_ext, partial, part_send, part_recv, asm, blk, coarse_ext,
    stat_send, stat_recv, bulk_send, bulk_recv, low_send, low_recv,
    red_send, red_recv, run_send, run_recv, far_send, far_recv, piece_send, top,
    via_bulk, via_stat, load_sem, inv_sem,
    lev_s, lev_r, part_s, part_r, coarse_s, coarse_r,
    stat_s, stat_r, bulk_s, bulk_r, low_s, low_r,
    via_s, via_r, red_s, red_r, asm_s, asm_r, run_s, run_r, far_s, far_r, top_s, top_r,
):
    x = lax.axis_index("gx")
    y = lax.axis_index("gy")
    rows, width = res.shape
    face = rows // 4
    primal = phi.shape[0]
    cdev, top_size = level.shape
    far_count = gx_count // RUN
    piece = top_size // gy_count
    pending = []

    def inside(a, b):
        ok_x = jnp.logical_and(x + a >= 0, x + a < gx_count)
        ok_y = jnp.logical_and(y + b >= 0, y + b < gy_count)
        return jnp.logical_and(ok_x, ok_y)

    def remote(src, dst, send, recv, dev):
        return pltpu.make_async_remote_copy(
            src_ref=src, dst_ref=dst, send_sem=send, recv_sem=recv,
            device_id=dev, device_id_type=MESH)

    def beside(a, b, src, dst, send, recv):
        @pl.when(inside(a, b))
        def _():
            remote(src, dst, send, recv, (x + a, y + b)).start()

        def done():
            @pl.when(inside(a, b))
            def _():
                remote(src, dst, send, recv, (x + a, y + b)).wait_send()
        pending.append(done)

    def arrived(a, b, dst, send, recv):
        @pl.when(inside(a, b))
        def _():
            remote(dst, dst, send, recv, (x + a, y + b)).wait_recv()

    def zero_outside(a, b, ref):
        @pl.when(jnp.logical_not(inside(a, b)))
        def _():
            ref[...] = jnp.zeros(ref.shape, ref.dtype)

    place = lax.rem(x, RUN)
    hop = jnp.where(place >= RUN // 2, 2, -2)
    third = x + hop
    has_third = jnp.logical_and(third >= 0, third < gx_count)
    passes_low = jnp.logical_and(place == 2, has_third)
    passes_high = jnp.logical_and(place == 1, has_third)

    def to_face(f, src, dst, send, recv, via, via_recv):
        a, b = FACES[f]
        if f > 1:
            beside(a, b, src, dst, send, recv)
            return
        last = place == (RUN - 1 if f == 1 else 0)
        ok = inside(a, b)

        @pl.when(jnp.logical_and(ok, jnp.logical_not(last)))
        def _():
            remote(src, dst, send, recv, (x + a, y)).start()

        @pl.when(jnp.logical_and(ok, last))
        def _():
            remote(src, via, send, via_recv, (x - a, y)).start()

        def done():
            @pl.when(ok)
            def _():
                remote(src, dst, send, recv, (x + a, y)).wait_send()
        pending.append(done)

    def pass_on(via, k, dst, recv):
        for slot, flag, a in ((0, passes_low, 2), (1, passes_high, -2)):
            @pl.when(flag)
            def _():
                remote(via, via, via_s.at[k], via_r.at[k], (x + a, y)).wait_recv()
                remote(via, dst(slot), via_s.at[k], recv(slot), (x + a, y)).start()

            def done(slot=slot, flag=flag, a=a):
                @pl.when(flag)
                def _():
                    remote(via, dst(slot), via_s.at[k], recv(slot), (x + a, y)).wait_send()
            pending.append(done)

    def gy_peer(d):
        return (x, lax.rem(y + d, gy_count))

    def run_peer(d):
        return (x - lax.rem(x, RUN) + lax.rem(lax.rem(x, RUN) + d, RUN), y)

    def far_peer(d):
        return (lax.rem(x // RUN + d, far_count) * RUN + lax.rem(x, RUN), y)

    def to_group(peer, d, src, dst, send, recv):
        remote(src, dst, send.at[d], recv.at[d], peer(d)).start()
        pending.append(lambda: remote(src, dst, send.at[d], recv.at[d], peer(d)).wait_send())

    def group_arrived(peer, d, dst, send, recv):
        remote(dst, dst, send.at[d], recv.at[d], peer(d)).wait_recv()

    loads = [
        pltpu.make_async_copy(src, dst, load_sem.at[i])
        for i, (src, dst) in enumerate([
            (level_h, level), (slots_h, slots), (sizes_h, sizes), (stiff_h, stiff),
            (topinv_h, topinv), (block_h, block), (phi_h, phi)])
    ]
    res_loads = [
        pltpu.make_async_copy(
            res_h.at[pl.ds(f * face, face)], res.at[pl.ds(f * face, face)],
            load_sem.at[len(loads) + f])
        for f in range(4)
    ]
    quarter = face // 4

    def quarter_rows(f, q):
        return pl.ds(f * face + q * quarter, quarter)

    inv_loads = [
        pltpu.make_async_copy(
            inv_h.at[quarter_rows(f, q)], inv.at[quarter_rows(f, q)], inv_sem.at[4 * q + f])
        for q in range(4) for f in range(4)
    ]
    for copy in loads + res_loads + inv_loads:
        copy.start()
    barrier = pltpu.get_barrier_semaphore()
    for a, b in OFFSETS:
        @pl.when(inside(a, b))
        def _():
            pl.semaphore_signal(barrier, inc=1, device_id=(x + a, y + b), device_id_type=MESH)
    @pl.when(has_third)
    def _():
        pl.semaphore_signal(barrier, inc=1, device_id=(third, y), device_id_type=MESH)
    for peer, count in ((gy_peer, gy_count), (run_peer, RUN), (far_peer, far_count)):
        for d in range(1, count):
            pl.semaphore_signal(barrier, inc=1, device_id=peer(d), device_id_type=MESH)

    for a, b in OFFSETS:
        zero_outside(a, b, lev_ext.at[slot_of(a, b)])
        zero_outside(a, b, part_recv.at[slot_of(a, b)])
        zero_outside(a, b, coarse_ext.at[slot_of(a, b)])
    for f, (a, b) in enumerate(FACES):
        zero_outside(a, b, stat_recv.at[f])
        zero_outside(a, b, bulk_recv.at[f])
        zero_outside(a, b, low_recv.at[f])

    for copy in loads:
        copy.wait()
    slot_row = jnp.broadcast_to(slots[...], (9 * cdev, primal))
    slot_iota = lax.broadcasted_iota(jnp.int32, (9 * cdev, primal), 0)
    sel_t = jnp.where(slot_row == slot_iota, 1.0, 0.0).astype(F32)
    sel_t16 = sel_t.astype(BF16)
    lev_ext[slot_of(0, 0)] = level[...]

    for f in range(4):
        res_loads[f].wait()
        live = lax.broadcasted_iota(jnp.int32, (face, width), 0) < sizes[0, f]
        part = res[pl.ds(f * face, face), :].astype(F32)
        masked[pl.ds(f * face, face), :] = jnp.where(live, part, 0.0).astype(BF16)
    partial[...] = dot(phi[...], masked[...])
    spread = dot(sel_t16, partial[...].astype(BF16))
    for k in range(9):
        part_send[k] = spread[k * cdev:(k + 1) * cdev].astype(BF16)
    def one(flag):
        return jnp.where(flag, 1, 0)

    count_x = 1 + one(x > 0) + one(x < gx_count - 1)
    count_y = 1 + one(y > 0) + one(y < gy_count - 1)
    pl.semaphore_wait(
        barrier, count_x * count_y - 1 + one(has_third) + gy_count - 1 + RUN - 1 + far_count - 1)

    for i, (a, b) in enumerate(OFFSETS):
        beside(a, b, level, lev_ext.at[slot_of(-a, -b)], lev_s.at[i], lev_r.at[slot_of(-a, -b)])

    for i, (a, b) in enumerate(OFFSETS):
        beside(a, b, part_send.at[slot_of(a, b)], part_recv.at[slot_of(-a, -b)],
               part_s.at[i], part_r.at[slot_of(-a, -b)])

    stiff32 = stiff[...].astype(F32)
    for f, (a, b) in enumerate(FACES):
        stat_send[f, :primal, :] = phi[:, f * face:(f + 1) * face]
        stat_send[f, primal:, :] = jnp.broadcast_to(
            stiff32[:, f * face:(f + 1) * face], (16, face)).astype(BF16)
        to_face(f, stat_send.at[f], stat_recv.at[f ^ 1], stat_s.at[f], stat_r.at[f ^ 1],
                via_stat, via_r.at[4])

    for f in range(4):
        lane = lax.broadcasted_iota(jnp.int32, (1, face), 1)
        weight = jnp.where(lane < sizes[0, f], stiff32[:, f * face:(f + 1) * face], 0.0)
        for j in range(face // 128):
            square = jnp.broadcast_to(weight[:, j * 128:(j + 1) * 128], (128, 128))
            col[pl.ds(f * face + j * 128, 128), :] = square.T

    def across(column):
        return jnp.concatenate([column] * (width // 128), axis=1)

    def multiply(q):
        for f in range(4):
            inv_loads[4 * q + f].wait()

        def step(p, carry):
            one_face = pl.multiple_of(2 * p * face + q * quarter, quarter)
            next_face = pl.multiple_of((2 * p + 1) * face + q * quarter, quarter)
            here, there = pl.ds(one_face, quarter), pl.ds(next_face, quarter)
            value = dot(jnp.concatenate([inv[here, :], inv[there, :]], axis=0), masked[...])
            scale = jnp.concatenate([col[here, :], col[there, :]], axis=0)
            value = (value * across(scale)).astype(BF16)
            bulk_send[2 * p, q * quarter:(q + 1) * quarter, :] = value[:quarter]
            bulk_send[2 * p + 1, q * quarter:(q + 1) * quarter, :] = value[quarter:]
            return carry

        lax.fori_loop(0, 2, step, 0)

    eighth = face // 8

    def send_eighth(e):
        part = pl.ds(e * eighth, eighth)
        for f, (a, b) in enumerate(FACES):
            ends = (bulk_send.at[f, part], bulk_recv.at[f ^ 1, part],
                    bulk_s.at[4 * e + f], bulk_r.at[4 * e + (f ^ 1)])
            if e < 4:
                to_face(f, *ends, via_bulk.at[e], via_r.at[e])
            else:
                beside(a, b, *ends)

    def pass_eighth(e):
        part = pl.ds(e * eighth, eighth)
        pass_on(via_bulk.at[e], e, lambda slot: bulk_recv.at[slot, part],
                lambda slot: bulk_r.at[4 * e + slot])

    multiply(0)
    send_eighth(0)

    for a, b in OFFSETS:
        arrived(a, b, lev_ext.at[slot_of(a, b)], lev_s.at[0], lev_r.at[slot_of(a, b)])
    lev_all = lev_ext[...].reshape(9 * cdev, top_size)
    basis = dot(sel_t, lev_all, ((0,), (0,)), HIGHEST)
    basis_inv = dot(basis, topinv[...], ((1,), (1,)), HIGHEST)
    share = dot(basis_inv, partial[...], ((0,), (0,)), HIGHEST)
    red_send[...] = share.reshape(gy_count, piece, width).astype(BF16)

    for d in range(1, gy_count):
        to_group(gy_peer, d, red_send.at[lax.rem(y + d, gy_count)],
                 red_recv.at[d], red_s, red_r)

    total = part_send[slot_of(0, 0)].astype(F32)
    for a, b in OFFSETS:
        arrived(a, b, part_recv.at[slot_of(a, b)], part_s.at[0], part_r.at[slot_of(a, b)])
        total = total + part_recv[slot_of(a, b)].astype(F32)
    asm[...] = total.astype(BF16)

    def block_rows(index):
        return pl.ds(pl.multiple_of(index * cdev, cdev), cdev)

    def swap_peer(d):
        return (x, y + 1 - 2 * lax.rem(y, 2))

    own_rows = block_rows(y)
    for d in range(2, gy_count, 2):
        to_group(gy_peer, d, asm, blk.at[own_rows], asm_s, asm_r)
    to_group(swap_peer, 1, asm, blk.at[own_rows], asm_s, asm_r)
    blk[own_rows, :] = total.astype(BF16)

    send_eighth(1)
    multiply(1)
    send_eighth(2)

    total = red_send[y].astype(F32)
    for d in range(1, gy_count):
        group_arrived(gy_peer, d, red_recv.at[d], red_s, red_r)
        total = total + red_recv[d].astype(F32)
    run_send[...] = total.astype(BF16)
    for d in range(1, RUN):
        to_group(run_peer, d, run_send, run_recv.at[d], run_s, run_r)

    send_eighth(3)
    pass_on(via_stat, 4, lambda slot: stat_recv.at[slot], lambda slot: stat_r.at[slot])
    pass_eighth(0)
    for d in range(2, gy_count, 2):
        group_arrived(gy_peer, d, asm, asm_s, asm_r)
        passed = blk.at[block_rows(lax.rem(y - d + gy_count, gy_count))]
        to_group(swap_peer, d + 1, passed, passed, asm_s, asm_r)
    for d in range(1, gy_count, 2):
        group_arrived(swap_peer, d, asm, asm_s, asm_r)
    coarse = dot(block[...], blk[...].astype(F32), precision=HIGHEST)
    coarse_ext[slot_of(0, 0)] = coarse.astype(BF16)
    for i, (a, b) in enumerate(OFFSETS):
        beside(a, b, coarse_ext.at[slot_of(0, 0)], coarse_ext.at[slot_of(-a, -b)],
               coarse_s.at[i], coarse_r.at[slot_of(-a, -b)])
    multiply(2)
    send_eighth(4)
    pass_eighth(1)

    total = run_send[...].astype(F32)
    for d in range(1, RUN):
        group_arrived(run_peer, d, run_recv.at[d], run_s, run_r)
        total = total + run_recv[d].astype(F32)
    far_send[...] = total.astype(BF16)
    for d in range(1, far_count):
        to_group(far_peer, d, far_send, far_recv.at[d], far_s, far_r)
    pass_eighth(2)
    send_eighth(5)
    multiply(3)
    send_eighth(6)
    pass_eighth(3)

    low_send[:, width:] = jnp.concatenate(
        [basis, jnp.zeros((primal, low_send.shape[1] - width - top_size), F32)], axis=1
    ).astype(BF16)
    for f, (a, b) in enumerate(FACES):
        arrived(a, b, stat_recv.at[f], stat_s.at[f], stat_r.at[f])
        lane = lax.broadcasted_iota(jnp.int32, (1, face), 1)
        live = lane < sizes[0, f]
        own = stiff32[:, f * face:(f + 1) * face]
        other = stat_recv[f, primal:primal + 16, :].astype(F32)[:1]
        scale = jnp.where(live, 1.0 / (own + other), 0.0)
        for j in range(face // 128):
            square = jnp.broadcast_to(scale[:, j * 128:(j + 1) * 128], (128, 128))
            dencol[pl.ds(f * face + j * 128, 128), :] = square.T
        own_phi = (stat_send[f, :primal, :].astype(F32) * (own * scale)).astype(BF16)
        other_phi = (stat_recv[f, :primal, :].astype(F32) * (other * scale)).astype(BF16)
        phit[pl.ds(f * face, face), :2 * primal] = jnp.concatenate([own_phi, other_phi], axis=0).T

    total = far_send[...].astype(F32)
    for d in range(1, far_count):
        group_arrived(far_peer, d, far_recv.at[d], far_s, far_r)
        total = total + far_recv[d].astype(F32)
    piece_send[...] = total.astype(BF16)
    for d in range(1, gy_count):
        to_group(gy_peer, d, piece_send, top.at[y], top_s, top_r)
    top[y] = total.astype(BF16)
    send_eighth(7)

    for a, b in OFFSETS:
        arrived(a, b, coarse_ext.at[slot_of(a, b)], coarse_s.at[0], coarse_r.at[slot_of(a, b)])
    ext = coarse_ext[...].reshape(9 * cdev, width)
    low_send[:, :width] = dot(sel_t16, ext, ((0,), (0,))).astype(BF16)
    for f, (a, b) in enumerate(FACES):
        beside(a, b, low_send, low_recv.at[f ^ 1], low_s.at[f], low_r.at[f ^ 1])
    low_out[...] = low_send[...]

    for q in range(4):
        part = pl.ds(q * quarter, quarter)
        for f, (a, b) in enumerate(FACES):
            for e in (2 * q, 2 * q + 1):
                rows_e = pl.ds(e * eighth, eighth)
                arrived(a, b, bulk_recv.at[f, rows_e], bulk_s.at[4 * e + f], bulk_r.at[4 * e + f])
            summed = bulk_send[f, part, :].astype(F32) + bulk_recv[f, part, :].astype(F32)
            acc[quarter_rows(f, q), :] = summed * across(dencol[quarter_rows(f, q), :])
    for f, (a, b) in enumerate(FACES):
        arrived(a, b, low_recv.at[f], low_s.at[f], low_r.at[f])
        lowr_out[f] = low_recv[f]
    for d in range(1, gy_count):
        group_arrived(gy_peer, d, top.at[0], top_s, top_r)
    top_out[...] = top[...].astype(F32).reshape(top_size, width)
    for done in pending:
        done()


def finish_kernel(acc, phit, low, lowr, top, out_h, out, sem):
    top_size, width = top.shape
    primal = low.shape[0]
    face = acc.shape[0] // 4
    top16 = top[...].astype(BF16)

    def full(value):
        lifted = dot(value[:, width:width + top_size], top16)
        return (value[:, :width].astype(F32) + lifted).astype(BF16)

    own = full(low[...])
    copies = []
    for f in range(4):
        both = jnp.concatenate([own, full(lowr[f])], axis=0)
        here = pl.ds(f * face, face)
        out[here, :] = (acc[here, :] + dot(phit[here, :2 * primal], both)).astype(BF16)
        copy = pltpu.make_async_copy(out.at[here], out_h.at[here], sem.at[f])
        copy.start()
        copies.append(copy)
    for copy in copies:
        copy.wait()


def local(gx_count, gy_count, residual, local_inverse, primal_basis, row_stiffness,
          face_sizes, primal_slots, block_inverse, level_basis, top_inverse):
    rows, width = residual.shape[2:]
    face = rows // 4
    primal = primal_basis.shape[2]
    cdev, top_size = level_basis.shape[2:]
    block_size = block_inverse.shape[3]
    far_count = gx_count // RUN
    piece = top_size // gy_count
    low_width = width + 128
    vm = pltpu.VMEM
    dma = pltpu.SemaphoreType.DMA
    args = (residual[0, 0], local_inverse[0, 0], primal_basis[0, 0], row_stiffness[0],
            face_sizes[0], primal_slots[0], block_inverse[0, 0], level_basis[0, 0], top_inverse)
    args = [pltpu.with_memory_space_constraint(arg, pltpu.MemorySpace.HBM) for arg in args]
    halo = dma((9,))
    four = dma((4,))
    gys = dma((gy_count,))
    scratch = [
        vm((rows, width), BF16), vm((rows, rows), BF16), vm((primal, rows), BF16),
        vm((1, rows), BF16), pltpu.SMEM((1, 4), jnp.int32), vm((1, primal), jnp.int32),
        vm((cdev, block_size), F32), vm((cdev, top_size), F32), vm((top_size, top_size), F32),
        vm((rows, width), BF16), vm((rows, 128), F32), vm((rows, 128), F32),
        vm((9, cdev, top_size), F32), vm((primal, width), F32),
        vm((9, cdev, width), BF16), vm((9, cdev, width), BF16),
        vm((cdev, width), BF16), vm((block_size, width), BF16), vm((9, cdev, width), BF16),
        vm((4, primal + 16, face), BF16), vm((4, primal + 16, face), BF16),
        vm((4, face, width), BF16), vm((4, face, width), BF16),
        vm((primal, low_width), BF16), vm((4, primal, low_width), BF16),
        vm((gy_count, piece, width), BF16), vm((gy_count, piece, width), BF16),
        vm((piece, width), BF16), vm((RUN, piece, width), BF16),
        vm((piece, width), BF16), vm((far_count, piece, width), BF16),
        vm((piece, width), BF16), vm((gy_count, piece, width), BF16),
        vm((4, face // 8, width), BF16), vm((primal + 16, face), BF16),
        dma((11,)), dma((16,)),
        halo, halo, halo, halo, halo, halo,
        four, four, dma((32,)), dma((32,)), four, four,
        dma((5,)), dma((5,)), gys, gys, gys, gys, dma((RUN,)), dma((RUN,)), dma((far_count,)), dma((far_count,)),
        gys, gys,
    ]
    kept = (
        vm((rows, width), F32), vm((rows, 256), BF16), vm((primal, low_width), BF16),
        vm((4, primal, low_width), BF16), vm((top_size, width), F32))
    values = pl.pallas_call(
        functools.partial(apply_kernel, gx_count, gy_count),
        name="apply",
        out_shape=kept,
        in_specs=[pl.BlockSpec(memory_space=pltpu.MemorySpace.HBM)] * len(args),
        out_specs=[pl.BlockSpec(memory_space=pltpu.MemorySpace.VMEM)] * len(kept),
        scratch_shapes=scratch,
        compiler_params=pltpu.CompilerParams(
            collective_id=0, has_side_effects=True, vmem_limit_bytes=40 << 20),
    )(*args)
    out = pl.pallas_call(
        finish_kernel,
        name="finish",
        out_shape=jax.ShapeDtypeStruct((rows, width), BF16),
        in_specs=[pl.BlockSpec(memory_space=pltpu.MemorySpace.VMEM)] * len(kept),
        out_specs=pl.BlockSpec(memory_space=pl.ANY),
        scratch_shapes=[vm((rows, width), BF16), dma((4,))],
        compiler_params=pltpu.CompilerParams(vmem_limit_bytes=16 << 20),
    )(*values)
    return out[None, None]


def solution(mesh):
    in_specs = (
        P("gx", "gy", None, None),
        P("gx", "gy", None, None),
        P("gx", "gy", None, None),
        P("gx", "gy", None),
        P("gx", "gy", None),
        P("gx", "gy", None),
        P("gx", "gy", None, None),
        P("gx", "gy", None, None),
        P(),
    )
    out_specs = P("gx", "gy", None, None)
    body = functools.partial(local, mesh.shape["gx"], mesh.shape["gy"])
    return jax.shard_map(body, mesh=mesh, in_specs=in_specs, out_specs=out_specs, check_vma=False)
```

```python
import functools

import jax
import jax.numpy as jnp
from jax import lax
from jax.experimental import pallas as pl
from jax.experimental.pallas import tpu as pltpu
from jax.sharding import PartitionSpec as P

MESH = pl.DeviceIdType.MESH
HIGHEST = lax.Precision.HIGHEST
F32 = jnp.float32
BF16 = jnp.bfloat16
RUN = 4
OFFSETS = [(a, b) for a in (-1, 0, 1) for b in (-1, 0, 1) if (a, b) != (0, 0)]
FACES = [(-1, 0), (1, 0), (0, -1), (0, 1)]


def dot(a, b, dims=((1,), (0,)), precision=None):
    return lax.dot_general(a, b, (dims, ((), ())), preferred_element_type=F32, precision=precision)


def slot_of(a, b):
    return (a + 1) * 3 + (b + 1)


def apply_kernel(
    gx_count,
    gy_count,
    res_h, inv_h, phi_h, stiff_h, sizes_h, slots_h, block_h, level_h, topinv_h,
    acc, phit, low_out, lowr_out, bas_out, basr_out, top_out,
    res, inv, phi, stiff, sizes, slots, block, level, topinv,
    masked, col, dencol, lev_ext, partial, part_send, part_recv, asm, blk, coarse_ext,
    stat_send, stat_recv, bulk_send, bulk_recv, low_send, low_recv,
    red_send, red_recv, run_send, run_recv, far_send, far_recv, piece_send, top,
    bas_send, bas_recv, via_bulk, via_stat, load_sem, inv_sem,
    lev_s, lev_r, part_s, part_r, coarse_s, coarse_r,
    stat_s, stat_r, bulk_s, bulk_r, low_s, low_r, bas_s, bas_r,
    via_s, via_r, red_s, red_r, asm_s, asm_r, run_s, run_r, far_s, far_r, top_s, top_r,
):
    x = lax.axis_index("gx")
    y = lax.axis_index("gy")
    rows, width = res.shape
    face = rows // 4
    primal = phi.shape[0]
    cdev, top_size = level.shape
    far_count = gx_count // RUN
    piece = top_size // gy_count
    pending = []

    def inside(a, b):
        ok_x = jnp.logical_and(x + a >= 0, x + a < gx_count)
        ok_y = jnp.logical_and(y + b >= 0, y + b < gy_count)
        return jnp.logical_and(ok_x, ok_y)

    def remote(src, dst, send, recv, dev):
        return pltpu.make_async_remote_copy(
            src_ref=src, dst_ref=dst, send_sem=send, recv_sem=recv,
            device_id=dev, device_id_type=MESH)

    def beside(a, b, src, dst, send, recv):
        @pl.when(inside(a, b))
        def _():
            remote(src, dst, send, recv, (x + a, y + b)).start()

        def done():
            @pl.when(inside(a, b))
            def _():
                remote(src, dst, send, recv, (x + a, y + b)).wait_send()
        pending.append(done)

    def arrived(a, b, dst, send, recv):
        @pl.when(inside(a, b))
        def _():
            remote(dst, dst, send, recv, (x + a, y + b)).wait_recv()

    def zero_outside(a, b, ref):
        @pl.when(jnp.logical_not(inside(a, b)))
        def _():
            ref[...] = jnp.zeros(ref.shape, ref.dtype)

    place = lax.rem(x, RUN)
    hop = jnp.where(place >= RUN // 2, 2, -2)
    third = x + hop
    has_third = jnp.logical_and(third >= 0, third < gx_count)
    passes_low = jnp.logical_and(place == 2, has_third)
    passes_high = jnp.logical_and(place == 1, has_third)

    def to_face(f, src, dst, send, recv, via, via_recv):
        a, b = FACES[f]
        if f > 1:
            beside(a, b, src, dst, send, recv)
            return
        last = place == (RUN - 1 if f == 1 else 0)
        ok = inside(a, b)

        @pl.when(jnp.logical_and(ok, jnp.logical_not(last)))
        def _():
            remote(src, dst, send, recv, (x + a, y)).start()

        @pl.when(jnp.logical_and(ok, last))
        def _():
            remote(src, via, send, via_recv, (x - a, y)).start()

        def done():
            @pl.when(ok)
            def _():
                remote(src, dst, send, recv, (x + a, y)).wait_send()
        pending.append(done)

    def pass_on(via, k, dst, recv):
        for slot, flag, a in ((0, passes_low, 2), (1, passes_high, -2)):
            @pl.when(flag)
            def _():
                remote(via, via, via_s.at[k], via_r.at[k], (x + a, y)).wait_recv()
                remote(via, dst(slot), via_s.at[k], recv(slot), (x + a, y)).start()

            def done(slot=slot, flag=flag, a=a):
                @pl.when(flag)
                def _():
                    remote(via, dst(slot), via_s.at[k], recv(slot), (x + a, y)).wait_send()
            pending.append(done)

    def gy_peer(d):
        return (x, lax.rem(y + d, gy_count))

    def run_peer(d):
        return (x - lax.rem(x, RUN) + lax.rem(lax.rem(x, RUN) + d, RUN), y)

    def far_peer(d):
        return (lax.rem(x // RUN + d, far_count) * RUN + lax.rem(x, RUN), y)

    def to_group(peer, d, src, dst, send, recv):
        remote(src, dst, send.at[d], recv.at[d], peer(d)).start()
        pending.append(lambda: remote(src, dst, send.at[d], recv.at[d], peer(d)).wait_send())

    def group_arrived(peer, d, dst, send, recv):
        remote(dst, dst, send.at[d], recv.at[d], peer(d)).wait_recv()

    loads = [
        pltpu.make_async_copy(src, dst, load_sem.at[i])
        for i, (src, dst) in enumerate([
            (level_h, level), (slots_h, slots), (sizes_h, sizes), (stiff_h, stiff),
            (topinv_h, topinv), (block_h, block), (phi_h, phi)])
    ]
    res_loads = [
        pltpu.make_async_copy(
            res_h.at[pl.ds(f * face, face)], res.at[pl.ds(f * face, face)],
            load_sem.at[len(loads) + f])
        for f in range(4)
    ]
    quarter = face // 4

    def quarter_rows(f, q):
        return pl.ds(f * face + q * quarter, quarter)

    inv_loads = [
        pltpu.make_async_copy(
            inv_h.at[quarter_rows(f, q)], inv.at[quarter_rows(f, q)], inv_sem.at[4 * q + f])
        for q in range(4) for f in range(4)
    ]
    for copy in loads + res_loads + inv_loads:
        copy.start()
    barrier = pltpu.get_barrier_semaphore()
    for a, b in OFFSETS:
        @pl.when(inside(a, b))
        def _():
            pl.semaphore_signal(barrier, inc=1, device_id=(x + a, y + b), device_id_type=MESH)
    @pl.when(has_third)
    def _():
        pl.semaphore_signal(barrier, inc=1, device_id=(third, y), device_id_type=MESH)
    for peer, count in ((gy_peer, gy_count), (run_peer, RUN), (far_peer, far_count)):
        for d in range(1, count):
            pl.semaphore_signal(barrier, inc=1, device_id=peer(d), device_id_type=MESH)

    for a, b in OFFSETS:
        zero_outside(a, b, lev_ext.at[slot_of(a, b)])
        zero_outside(a, b, part_recv.at[slot_of(a, b)])
        zero_outside(a, b, coarse_ext.at[slot_of(a, b)])
    for f, (a, b) in enumerate(FACES):
        zero_outside(a, b, stat_recv.at[f])
        zero_outside(a, b, bulk_recv.at[f])
        zero_outside(a, b, low_recv.at[f])
        zero_outside(a, b, bas_recv.at[f])

    for copy in loads:
        copy.wait()
    slot_row = jnp.broadcast_to(slots[...], (9 * cdev, primal))
    slot_iota = lax.broadcasted_iota(jnp.int32, (9 * cdev, primal), 0)
    sel_t = jnp.where(slot_row == slot_iota, 1.0, 0.0).astype(F32)
    sel_t16 = sel_t.astype(BF16)
    lev_ext[slot_of(0, 0)] = level[...]
    lift = dot(topinv[...], level[...], ((1,), (1,)), HIGHEST)

    for f in range(4):
        res_loads[f].wait()
        live = lax.broadcasted_iota(jnp.int32, (face, width), 0) < sizes[0, f]
        part = res[pl.ds(f * face, face), :].astype(F32)
        masked[pl.ds(f * face, face), :] = jnp.where(live, part, 0.0).astype(BF16)
    partial[...] = dot(phi[...], masked[...])
    spread = dot(sel_t16, partial[...].astype(BF16))
    for k in range(9):
        part_send[k] = spread[k * cdev:(k + 1) * cdev].astype(BF16)
    def one(flag):
        return jnp.where(flag, 1, 0)

    count_x = 1 + one(x > 0) + one(x < gx_count - 1)
    count_y = 1 + one(y > 0) + one(y < gy_count - 1)
    pl.semaphore_wait(
        barrier, count_x * count_y - 1 + one(has_third) + gy_count - 1 + RUN - 1 + far_count - 1)

    for i, (a, b) in enumerate(OFFSETS):
        beside(a, b, part_send.at[slot_of(a, b)], part_recv.at[slot_of(-a, -b)],
               part_s.at[i], part_r.at[slot_of(-a, -b)])
    for i, (a, b) in enumerate(OFFSETS):
        beside(a, b, level, lev_ext.at[slot_of(-a, -b)], lev_s.at[i], lev_r.at[slot_of(-a, -b)])

    stiff32 = stiff[...].astype(F32)
    for f, (a, b) in enumerate(FACES):
        stat_send[f, :primal, :] = phi[:, f * face:(f + 1) * face]
        stat_send[f, primal:, :] = jnp.broadcast_to(
            stiff32[:, f * face:(f + 1) * face], (16, face)).astype(BF16)
        to_face(f, stat_send.at[f], stat_recv.at[f ^ 1], stat_s.at[f], stat_r.at[f ^ 1],
                via_stat, via_r.at[4])

    for f in range(4):
        lane = lax.broadcasted_iota(jnp.int32, (1, face), 1)
        weight = jnp.where(lane < sizes[0, f], stiff32[:, f * face:(f + 1) * face], 0.0)
        for j in range(face // 128):
            square = jnp.broadcast_to(weight[:, j * 128:(j + 1) * 128], (128, 128))
            col[pl.ds(f * face + j * 128, 128), :] = square.T

    def across(column):
        return jnp.concatenate([column] * (width // 128), axis=1)

    def multiply(q):
        for f in range(4):
            inv_loads[4 * q + f].wait()

        def step(p, carry):
            one_face = pl.multiple_of(2 * p * face + q * quarter, quarter)
            next_face = pl.multiple_of((2 * p + 1) * face + q * quarter, quarter)
            here, there = pl.ds(one_face, quarter), pl.ds(next_face, quarter)
            value = dot(jnp.concatenate([inv[here, :], inv[there, :]], axis=0), masked[...])
            scale = jnp.concatenate([col[here, :], col[there, :]], axis=0)
            value = (value * across(scale)).astype(BF16)
            bulk_send[2 * p, q * quarter:(q + 1) * quarter, :] = value[:quarter]
            bulk_send[2 * p + 1, q * quarter:(q + 1) * quarter, :] = value[quarter:]
            return carry

        lax.fori_loop(0, 2, step, 0)

    eighth = face // 8

    def send_eighth(e):
        part = pl.ds(e * eighth, eighth)
        for f, (a, b) in enumerate(FACES):
            ends = (bulk_send.at[f, part], bulk_recv.at[f ^ 1, part],
                    bulk_s.at[4 * e + f], bulk_r.at[4 * e + (f ^ 1)])
            if e < 4:
                to_face(f, *ends, via_bulk.at[e], via_r.at[e])
            else:
                beside(a, b, *ends)

    def pass_eighth(e):
        part = pl.ds(e * eighth, eighth)
        pass_on(via_bulk.at[e], e, lambda slot: bulk_recv.at[slot, part],
                lambda slot: bulk_r.at[4 * e + slot])

    multiply(0)
    send_eighth(0)
    multiply(1)

    total = part_send[slot_of(0, 0)].astype(F32)
    for a, b in OFFSETS:
        arrived(a, b, part_recv.at[slot_of(a, b)], part_s.at[0], part_r.at[slot_of(a, b)])
        total = total + part_recv[slot_of(a, b)].astype(F32)
    share = dot(lift, total, precision=HIGHEST)
    red_send[...] = share.reshape(gy_count, piece, width).astype(BF16)

    for d in range(1, gy_count):
        to_group(gy_peer, d, red_send.at[lax.rem(y + d, gy_count)],
                 red_recv.at[d], red_s, red_r)
    asm[...] = total.astype(BF16)

    def block_rows(index):
        return pl.ds(pl.multiple_of(index * cdev, cdev), cdev)

    def swap_peer(d):
        return (x, y + 1 - 2 * lax.rem(y, 2))

    own_rows = block_rows(y)
    for d in range(2, gy_count, 2):
        to_group(gy_peer, d, asm, blk.at[own_rows], asm_s, asm_r)
    to_group(swap_peer, 1, asm, blk.at[own_rows], asm_s, asm_r)
    blk[own_rows, :] = total.astype(BF16)

    for a, b in OFFSETS:
        arrived(a, b, lev_ext.at[slot_of(a, b)], lev_s.at[0], lev_r.at[slot_of(a, b)])
    lev_all = lev_ext[...].reshape(9 * cdev, top_size)
    basis = dot(sel_t, lev_all, ((0,), (0,)), HIGHEST)
    bas_send[...] = jnp.concatenate(
        [basis, jnp.zeros((primal, bas_send.shape[1] - top_size), F32)], axis=1).astype(BF16)
    for f, (a, b) in enumerate(FACES):
        beside(a, b, bas_send, bas_recv.at[f ^ 1], bas_s.at[f], bas_r.at[f ^ 1])
    send_eighth(1)
    send_eighth(2)
    multiply(2)

    total = red_send[y].astype(F32)
    for d in range(1, gy_count):
        group_arrived(gy_peer, d, red_recv.at[d], red_s, red_r)
        total = total + red_recv[d].astype(F32)
    run_send[...] = total.astype(BF16)
    for d in range(1, RUN):
        to_group(run_peer, d, run_send, run_recv.at[d], run_s, run_r)

    send_eighth(3)
    pass_on(via_stat, 4, lambda slot: stat_recv.at[slot], lambda slot: stat_r.at[slot])
    pass_eighth(0)
    for d in range(2, gy_count, 2):
        group_arrived(gy_peer, d, asm, asm_s, asm_r)
        passed = blk.at[block_rows(lax.rem(y - d + gy_count, gy_count))]
        to_group(swap_peer, d + 1, passed, passed, asm_s, asm_r)
    for d in range(1, gy_count, 2):
        group_arrived(swap_peer, d, asm, asm_s, asm_r)
    coarse = dot(block[...], blk[...].astype(F32), precision=HIGHEST)
    coarse_ext[slot_of(0, 0)] = coarse.astype(BF16)
    for i, (a, b) in enumerate(OFFSETS):
        beside(a, b, coarse_ext.at[slot_of(0, 0)], coarse_ext.at[slot_of(-a, -b)],
               coarse_s.at[i], coarse_r.at[slot_of(-a, -b)])
    send_eighth(4)
    multiply(3)
    send_eighth(5)
    pass_eighth(1)

    total = run_send[...].astype(F32)
    for d in range(1, RUN):
        group_arrived(run_peer, d, run_recv.at[d], run_s, run_r)
        total = total + run_recv[d].astype(F32)
    far_send[...] = total.astype(BF16)
    for d in range(1, far_count):
        to_group(far_peer, d, far_send, far_recv.at[d], far_s, far_r)
    send_eighth(6)
    pass_eighth(2)
    pass_eighth(3)
    send_eighth(7)

    bas_out[...] = bas_send[...]
    for f, (a, b) in enumerate(FACES):
        arrived(a, b, stat_recv.at[f], stat_s.at[f], stat_r.at[f])
        arrived(a, b, bas_recv.at[f], bas_s.at[f], bas_r.at[f])
        basr_out[f] = bas_recv[f]
        lane = lax.broadcasted_iota(jnp.int32, (1, face), 1)
        live = lane < sizes[0, f]
        own = stiff32[:, f * face:(f + 1) * face]
        other = stat_recv[f, primal:primal + 16, :].astype(F32)[:1]
        scale = jnp.where(live, 1.0 / (own + other), 0.0)
        for j in range(face // 128):
            square = jnp.broadcast_to(scale[:, j * 128:(j + 1) * 128], (128, 128))
            dencol[pl.ds(f * face + j * 128, 128), :] = square.T
        own_phi = (stat_send[f, :primal, :].astype(F32) * (own * scale)).astype(BF16)
        other_phi = (stat_recv[f, :primal, :].astype(F32) * (other * scale)).astype(BF16)
        phit[pl.ds(f * face, face), :2 * primal] = jnp.concatenate([own_phi, other_phi], axis=0).T

    for a, b in OFFSETS:
        arrived(a, b, coarse_ext.at[slot_of(a, b)], coarse_s.at[0], coarse_r.at[slot_of(a, b)])
    ext = coarse_ext[...].reshape(9 * cdev, width)
    low_send[...] = dot(sel_t16, ext, ((0,), (0,))).astype(BF16)
    for f, (a, b) in enumerate(FACES):
        beside(a, b, low_send, low_recv.at[f ^ 1], low_s.at[f], low_r.at[f ^ 1])
    total = far_send[...].astype(F32)
    for d in range(1, far_count):
        group_arrived(far_peer, d, far_recv.at[d], far_s, far_r)
        total = total + far_recv[d].astype(F32)
    piece_send[...] = total.astype(BF16)
    for d in range(1, gy_count):
        to_group(gy_peer, d, piece_send, top.at[y], top_s, top_r)
    top[y] = total.astype(BF16)

    low_out[...] = low_send[...]

    for q in range(4):
        part = pl.ds(q * quarter, quarter)
        for f, (a, b) in enumerate(FACES):
            for e in (2 * q, 2 * q + 1):
                rows_e = pl.ds(e * eighth, eighth)
                arrived(a, b, bulk_recv.at[f, rows_e], bulk_s.at[4 * e + f], bulk_r.at[4 * e + f])
            summed = bulk_send[f, part, :].astype(F32) + bulk_recv[f, part, :].astype(F32)
            acc[quarter_rows(f, q), :] = summed * across(dencol[quarter_rows(f, q), :])
    for done in pending:
        done()
    for f, (a, b) in enumerate(FACES):
        arrived(a, b, low_recv.at[f], low_s.at[f], low_r.at[f])
        lowr_out[f] = low_recv[f]
    for d in range(1, gy_count):
        group_arrived(gy_peer, d, top.at[0], top_s, top_r)
    top_out[...] = top[...].astype(F32).reshape(top_size, width)


def finish_kernel(acc, phit, low, lowr, bas, basr, top, out_h, out, sem):
    top_size = top.shape[0]
    primal = low.shape[0]
    face = acc.shape[0] // 4
    top16 = top[...].astype(BF16)

    def full(value, basis):
        return (value.astype(F32) + dot(basis[:, :top_size], top16)).astype(BF16)

    own = full(low[...], bas[...])
    copies = []
    for f in range(4):
        both = jnp.concatenate([own, full(lowr[f], basr[f])], axis=0)
        here = pl.ds(f * face, face)
        out[here, :] = (acc[here, :] + dot(phit[here, :2 * primal], both)).astype(BF16)
        copy = pltpu.make_async_copy(out.at[here], out_h.at[here], sem.at[f])
        copy.start()
        copies.append(copy)
    for copy in copies:
        copy.wait()


def local(gx_count, gy_count, residual, local_inverse, primal_basis, row_stiffness,
          face_sizes, primal_slots, block_inverse, level_basis, top_inverse):
    rows, width = residual.shape[2:]
    face = rows // 4
    primal = primal_basis.shape[2]
    cdev, top_size = level_basis.shape[2:]
    block_size = block_inverse.shape[3]
    far_count = gx_count // RUN
    piece = top_size // gy_count
    vm = pltpu.VMEM
    dma = pltpu.SemaphoreType.DMA
    args = (residual[0, 0], local_inverse[0, 0], primal_basis[0, 0], row_stiffness[0],
            face_sizes[0], primal_slots[0], block_inverse[0, 0], level_basis[0, 0], top_inverse)
    args = [pltpu.with_memory_space_constraint(arg, pltpu.MemorySpace.HBM) for arg in args]
    halo = dma((9,))
    four = dma((4,))
    gys = dma((gy_count,))
    scratch = [
        vm((rows, width), BF16), vm((rows, rows), BF16), vm((primal, rows), BF16),
        vm((1, rows), BF16), pltpu.SMEM((1, 4), jnp.int32), vm((1, primal), jnp.int32),
        vm((cdev, block_size), F32), vm((cdev, top_size), F32), vm((top_size, top_size), F32),
        vm((rows, width), BF16), vm((rows, 128), F32), vm((rows, 128), F32),
        vm((9, cdev, top_size), F32), vm((primal, width), F32),
        vm((9, cdev, width), BF16), vm((9, cdev, width), BF16),
        vm((cdev, width), BF16), vm((block_size, width), BF16), vm((9, cdev, width), BF16),
        vm((4, primal + 16, face), BF16), vm((4, primal + 16, face), BF16),
        vm((4, face, width), BF16), vm((4, face, width), BF16),
        vm((primal, width), BF16), vm((4, primal, width), BF16),
        vm((gy_count, piece, width), BF16), vm((gy_count, piece, width), BF16),
        vm((piece, width), BF16), vm((RUN, piece, width), BF16),
        vm((piece, width), BF16), vm((far_count, piece, width), BF16),
        vm((piece, width), BF16), vm((gy_count, piece, width), BF16),
        vm((primal, 128), BF16), vm((4, primal, 128), BF16),
        vm((4, face // 8, width), BF16), vm((primal + 16, face), BF16),
        dma((11,)), dma((16,)),
        halo, halo, halo, halo, halo, halo,
        four, four, dma((32,)), dma((32,)), four, four, four, four,
        dma((5,)), dma((5,)), gys, gys, gys, gys, dma((RUN,)), dma((RUN,)), dma((far_count,)), dma((far_count,)),
        gys, gys,
    ]
    kept = (
        vm((rows, width), F32), vm((rows, 256), BF16), vm((primal, width), BF16),
        vm((4, primal, width), BF16), vm((primal, 128), BF16), vm((4, primal, 128), BF16),
        vm((top_size, width), F32))
    values = pl.pallas_call(
        functools.partial(apply_kernel, gx_count, gy_count),
        name="apply",
        out_shape=kept,
        in_specs=[pl.BlockSpec(memory_space=pltpu.MemorySpace.HBM)] * len(args),
        out_specs=[pl.BlockSpec(memory_space=pltpu.MemorySpace.VMEM)] * len(kept),
        scratch_shapes=scratch,
        compiler_params=pltpu.CompilerParams(
            collective_id=0, has_side_effects=True, vmem_limit_bytes=40 << 20),
    )(*args)
    out = pl.pallas_call(
        finish_kernel,
        name="finish",
        out_shape=jax.ShapeDtypeStruct((rows, width), BF16),
        in_specs=[pl.BlockSpec(memory_space=pltpu.MemorySpace.VMEM)] * len(kept),
        out_specs=pl.BlockSpec(memory_space=pl.ANY),
        scratch_shapes=[vm((rows, width), BF16), dma((4,))],
        compiler_params=pltpu.CompilerParams(vmem_limit_bytes=16 << 20),
    )(*values)
    return out[None, None]


def solution(mesh):
    in_specs = (
        P("gx", "gy", None, None),
        P("gx", "gy", None, None),
        P("gx", "gy", None, None),
        P("gx", "gy", None),
        P("gx", "gy", None),
        P("gx", "gy", None),
        P("gx", "gy", None, None),
        P("gx", "gy", None, None),
        P(),
    )
    out_specs = P("gx", "gy", None, None)
    body = functools.partial(local, mesh.shape["gx"], mesh.shape["gy"])
    return jax.shard_map(body, mesh=mesh, in_specs=in_specs, out_specs=out_specs, check_vma=False)
```

```python
import functools

import jax
import jax.numpy as jnp
from jax import lax
from jax.experimental import pallas as pl
from jax.experimental.pallas import tpu as pltpu
from jax.sharding import PartitionSpec as P

MESH = pl.DeviceIdType.MESH
HIGHEST = lax.Precision.HIGHEST
F32 = jnp.float32
BF16 = jnp.bfloat16
RUN = 4
OFFSETS = [(a, b) for a in (-1, 0, 1) for b in (-1, 0, 1) if (a, b) != (0, 0)]
FACES = [(-1, 0), (1, 0), (0, -1), (0, 1)]


def dot(a, b, dims=((1,), (0,)), precision=None):
    return lax.dot_general(a, b, (dims, ((), ())), preferred_element_type=F32, precision=precision)


def slot_of(a, b):
    return (a + 1) * 3 + (b + 1)


def apply_kernel(
    gx_count,
    gy_count,
    res_h, inv_h, phi_h, stiff_h, sizes_h, slots_h, block_h, level_h, topinv_h,
    acc, phit, low_out, lowr_out, bas_out, basr_out, top_out,
    res, inv, phi, stiff, sizes, slots, block, level, topinv,
    masked, col, dencol, lev_ext, partial, part_send, part_recv, asm, blk, coarse_ext,
    stat_send, stat_recv, bulk_send, bulk_recv, low_send, low_recv,
    red_send, red_recv, run_send, run_recv, far_send, far_recv, piece_send, top,
    bas_send, bas_recv, via_bulk, via_stat, load_sem, inv_sem,
    lev_s, lev_r, part_s, part_r, coarse_s, coarse_r,
    stat_s, stat_r, bulk_s, bulk_r, low_s, low_r, bas_s, bas_r,
    via_s, via_r, red_s, red_r, asm_s, asm_r, run_s, run_r, far_s, far_r, top_s, top_r,
):
    x = lax.axis_index("gx")
    y = lax.axis_index("gy")
    rows, width = res.shape
    face = rows // 4
    primal = phi.shape[0]
    cdev, top_size = level.shape
    far_count = gx_count // RUN
    piece = top_size // gy_count
    pending = []

    def inside(a, b):
        ok_x = jnp.logical_and(x + a >= 0, x + a < gx_count)
        ok_y = jnp.logical_and(y + b >= 0, y + b < gy_count)
        return jnp.logical_and(ok_x, ok_y)

    def remote(src, dst, send, recv, dev):
        return pltpu.make_async_remote_copy(
            src_ref=src, dst_ref=dst, send_sem=send, recv_sem=recv,
            device_id=dev, device_id_type=MESH)

    def beside(a, b, src, dst, send, recv):
        @pl.when(inside(a, b))
        def _():
            remote(src, dst, send, recv, (x + a, y + b)).start()

        def done():
            @pl.when(inside(a, b))
            def _():
                remote(src, dst, send, recv, (x + a, y + b)).wait_send()
        pending.append(done)

    def arrived(a, b, dst, send, recv):
        @pl.when(inside(a, b))
        def _():
            remote(dst, dst, send, recv, (x + a, y + b)).wait_recv()

    def zero_outside(a, b, ref):
        @pl.when(jnp.logical_not(inside(a, b)))
        def _():
            ref[...] = jnp.zeros(ref.shape, ref.dtype)

    place = lax.rem(x, RUN)
    hop = jnp.where(place >= RUN // 2, 2, -2)
    third = x + hop
    has_third = jnp.logical_and(third >= 0, third < gx_count)
    passes_low = jnp.logical_and(place == 2, has_third)
    passes_high = jnp.logical_and(place == 1, has_third)

    def to_face(f, src, dst, send, recv, via, via_recv):
        a, b = FACES[f]
        if f > 1:
            beside(a, b, src, dst, send, recv)
            return
        last = place == (RUN - 1 if f == 1 else 0)
        ok = inside(a, b)

        @pl.when(jnp.logical_and(ok, jnp.logical_not(last)))
        def _():
            remote(src, dst, send, recv, (x + a, y)).start()

        @pl.when(jnp.logical_and(ok, last))
        def _():
            remote(src, via, send, via_recv, (x - a, y)).start()

        def done():
            @pl.when(ok)
            def _():
                remote(src, dst, send, recv, (x + a, y)).wait_send()
        pending.append(done)

    def pass_on(via, k, dst, recv):
        for slot, flag, a in ((0, passes_low, 2), (1, passes_high, -2)):
            @pl.when(flag)
            def _():
                remote(via, via, via_s.at[k], via_r.at[k], (x + a, y)).wait_recv()
                remote(via, dst(slot), via_s.at[k], recv(slot), (x + a, y)).start()

            def done(slot=slot, flag=flag, a=a):
                @pl.when(flag)
                def _():
                    remote(via, dst(slot), via_s.at[k], recv(slot), (x + a, y)).wait_send()
            pending.append(done)

    def gy_peer(d):
        return (x, lax.rem(y + d, gy_count))

    def run_peer(d):
        return (x - lax.rem(x, RUN) + lax.rem(lax.rem(x, RUN) + d, RUN), y)

    def far_peer(d):
        return (lax.rem(x // RUN + d, far_count) * RUN + lax.rem(x, RUN), y)

    def to_group(peer, d, src, dst, send, recv):
        remote(src, dst, send.at[d], recv.at[d], peer(d)).start()
        pending.append(lambda: remote(src, dst, send.at[d], recv.at[d], peer(d)).wait_send())

    def group_arrived(peer, d, dst, send, recv):
        remote(dst, dst, send.at[d], recv.at[d], peer(d)).wait_recv()

    loads = [
        pltpu.make_async_copy(src, dst, load_sem.at[i])
        for i, (src, dst) in enumerate([
            (level_h, level), (slots_h, slots), (sizes_h, sizes), (stiff_h, stiff),
            (topinv_h, topinv), (block_h, block), (phi_h, phi)])
    ]
    res_loads = [
        pltpu.make_async_copy(
            res_h.at[pl.ds(f * face, face)], res.at[pl.ds(f * face, face)],
            load_sem.at[len(loads) + f])
        for f in range(4)
    ]
    quarter = face // 4

    def quarter_rows(f, q):
        return pl.ds(f * face + q * quarter, quarter)

    inv_loads = [
        pltpu.make_async_copy(
            inv_h.at[quarter_rows(f, q)], inv.at[quarter_rows(f, q)], inv_sem.at[4 * q + f])
        for q in range(4) for f in range(4)
    ]
    for copy in loads + res_loads + inv_loads:
        copy.start()
    barrier = pltpu.get_barrier_semaphore()
    for a, b in OFFSETS:
        @pl.when(inside(a, b))
        def _():
            pl.semaphore_signal(barrier, inc=1, device_id=(x + a, y + b), device_id_type=MESH)
    @pl.when(has_third)
    def _():
        pl.semaphore_signal(barrier, inc=1, device_id=(third, y), device_id_type=MESH)
    for peer, count in ((gy_peer, gy_count), (run_peer, RUN), (far_peer, far_count)):
        for d in range(1, count):
            pl.semaphore_signal(barrier, inc=1, device_id=peer(d), device_id_type=MESH)

    for a, b in OFFSETS:
        zero_outside(a, b, lev_ext.at[slot_of(a, b)])
        zero_outside(a, b, part_recv.at[slot_of(a, b)])
        zero_outside(a, b, coarse_ext.at[slot_of(a, b)])
    for f, (a, b) in enumerate(FACES):
        zero_outside(a, b, stat_recv.at[f])
        zero_outside(a, b, bulk_recv.at[f])
        zero_outside(a, b, low_recv.at[f])
        zero_outside(a, b, bas_recv.at[f])

    for copy in loads:
        copy.wait()
    slot_row = jnp.broadcast_to(slots[...], (9 * cdev, primal))
    slot_iota = lax.broadcasted_iota(jnp.int32, (9 * cdev, primal), 0)
    sel_t = jnp.where(slot_row == slot_iota, 1.0, 0.0).astype(F32)
    sel_t16 = sel_t.astype(BF16)
    lev_ext[slot_of(0, 0)] = level[...]
    block_high = block[...].astype(BF16)
    block_low = (block[...] - block_high.astype(F32)).astype(BF16)
    lift = dot(topinv[...], level[...], ((1,), (1,)), HIGHEST)

    for f in range(4):
        res_loads[f].wait()
        live = lax.broadcasted_iota(jnp.int32, (face, width), 0) < sizes[0, f]
        part = res[pl.ds(f * face, face), :].astype(F32)
        masked[pl.ds(f * face, face), :] = jnp.where(live, part, 0.0).astype(BF16)
    partial[...] = dot(phi[...], masked[...])
    spread = dot(sel_t16, partial[...].astype(BF16))
    for k in range(9):
        part_send[k] = spread[k * cdev:(k + 1) * cdev].astype(BF16)
    def one(flag):
        return jnp.where(flag, 1, 0)

    count_x = 1 + one(x > 0) + one(x < gx_count - 1)
    count_y = 1 + one(y > 0) + one(y < gy_count - 1)
    pl.semaphore_wait(
        barrier, count_x * count_y - 1 + one(has_third) + gy_count - 1 + RUN - 1 + far_count - 1)

    for i, (a, b) in enumerate(OFFSETS):
        beside(a, b, part_send.at[slot_of(a, b)], part_recv.at[slot_of(-a, -b)],
               part_s.at[i], part_r.at[slot_of(-a, -b)])
    for i, (a, b) in enumerate(OFFSETS):
        beside(a, b, level, lev_ext.at[slot_of(-a, -b)], lev_s.at[i], lev_r.at[slot_of(-a, -b)])

    stiff32 = stiff[...].astype(F32)
    for f, (a, b) in enumerate(FACES):
        stat_send[f, :primal, :] = phi[:, f * face:(f + 1) * face]
        stat_send[f, primal:, :] = jnp.broadcast_to(
            stiff32[:, f * face:(f + 1) * face], (16, face)).astype(BF16)
        to_face(f, stat_send.at[f], stat_recv.at[f ^ 1], stat_s.at[f], stat_r.at[f ^ 1],
                via_stat, via_r.at[4])

    for f in range(4):
        lane = lax.broadcasted_iota(jnp.int32, (1, face), 1)
        weight = jnp.where(lane < sizes[0, f], stiff32[:, f * face:(f + 1) * face], 0.0)
        for j in range(face // 128):
            square = jnp.broadcast_to(weight[:, j * 128:(j + 1) * 128], (128, 128))
            col[pl.ds(f * face + j * 128, 128), :] = square.T

    def across(column):
        return jnp.concatenate([column] * (width // 128), axis=1)

    def multiply(q):
        for f in range(4):
            inv_loads[4 * q + f].wait()

        def step(p, carry):
            one_face = pl.multiple_of(2 * p * face + q * quarter, quarter)
            next_face = pl.multiple_of((2 * p + 1) * face + q * quarter, quarter)
            here, there = pl.ds(one_face, quarter), pl.ds(next_face, quarter)
            value = dot(jnp.concatenate([inv[here, :], inv[there, :]], axis=0), masked[...])
            scale = jnp.concatenate([col[here, :], col[there, :]], axis=0)
            value = (value * across(scale)).astype(BF16)
            bulk_send[2 * p, q * quarter:(q + 1) * quarter, :] = value[:quarter]
            bulk_send[2 * p + 1, q * quarter:(q + 1) * quarter, :] = value[quarter:]
            return carry

        lax.fori_loop(0, 2, step, 0)

    eighth = face // 8

    def send_eighth(e):
        part = pl.ds(e * eighth, eighth)
        for f, (a, b) in enumerate(FACES):
            ends = (bulk_send.at[f, part], bulk_recv.at[f ^ 1, part],
                    bulk_s.at[4 * e + f], bulk_r.at[4 * e + (f ^ 1)])
            if e < 4:
                to_face(f, *ends, via_bulk.at[e], via_r.at[e])
            else:
                beside(a, b, *ends)

    def pass_eighth(e):
        part = pl.ds(e * eighth, eighth)
        pass_on(via_bulk.at[e], e, lambda slot: bulk_recv.at[slot, part],
                lambda slot: bulk_r.at[4 * e + slot])

    multiply(0)
    send_eighth(0)
    multiply(1)

    total = part_send[slot_of(0, 0)].astype(F32)
    for a, b in OFFSETS:
        arrived(a, b, part_recv.at[slot_of(a, b)], part_s.at[0], part_r.at[slot_of(a, b)])
        total = total + part_recv[slot_of(a, b)].astype(F32)
    share = dot(lift, total, precision=HIGHEST)
    red_send[...] = share.reshape(gy_count, piece, width).astype(BF16)

    for d in range(1, gy_count):
        to_group(gy_peer, d, red_send.at[lax.rem(y + d, gy_count)],
                 red_recv.at[d], red_s, red_r)
    asm[...] = total.astype(BF16)

    def block_rows(index):
        return pl.ds(pl.multiple_of(index * cdev, cdev), cdev)

    def swap_peer(d):
        return (x, y + 1 - 2 * lax.rem(y, 2))

    own_rows = block_rows(y)
    for d in range(2, gy_count, 2):
        to_group(gy_peer, d, asm, blk.at[own_rows], asm_s, asm_r)
    to_group(swap_peer, 1, asm, blk.at[own_rows], asm_s, asm_r)
    blk[own_rows, :] = total.astype(BF16)

    for a, b in OFFSETS:
        arrived(a, b, lev_ext.at[slot_of(a, b)], lev_s.at[0], lev_r.at[slot_of(a, b)])
    lev_all = lev_ext[...].reshape(9 * cdev, top_size)
    basis = dot(sel_t, lev_all, ((0,), (0,)), HIGHEST)
    bas_send[...] = jnp.concatenate(
        [basis, jnp.zeros((primal, bas_send.shape[1] - top_size), F32)], axis=1).astype(BF16)
    for f, (a, b) in enumerate(FACES):
        beside(a, b, bas_send, bas_recv.at[f ^ 1], bas_s.at[f], bas_r.at[f ^ 1])
    send_eighth(1)
    send_eighth(2)
    multiply(2)

    total = red_send[y].astype(F32)
    for d in range(1, gy_count):
        group_arrived(gy_peer, d, red_recv.at[d], red_s, red_r)
        total = total + red_recv[d].astype(F32)
    run_send[...] = total.astype(BF16)
    for d in range(1, RUN):
        to_group(run_peer, d, run_send, run_recv.at[d], run_s, run_r)

    send_eighth(3)
    pass_on(via_stat, 4, lambda slot: stat_recv.at[slot], lambda slot: stat_r.at[slot])
    pass_eighth(0)
    for d in range(2, gy_count, 2):
        group_arrived(gy_peer, d, asm, asm_s, asm_r)
        passed = blk.at[block_rows(lax.rem(y - d + gy_count, gy_count))]
        to_group(swap_peer, d + 1, passed, passed, asm_s, asm_r)
    for d in range(1, gy_count, 2):
        group_arrived(swap_peer, d, asm, asm_s, asm_r)
    coarse = dot(block_high, blk[...]) + dot(block_low, blk[...])
    coarse_ext[slot_of(0, 0)] = coarse.astype(BF16)
    for i, (a, b) in enumerate(OFFSETS):
        beside(a, b, coarse_ext.at[slot_of(0, 0)], coarse_ext.at[slot_of(-a, -b)],
               coarse_s.at[i], coarse_r.at[slot_of(-a, -b)])
    send_eighth(4)
    multiply(3)
    send_eighth(5)
    pass_eighth(1)

    total = run_send[...].astype(F32)
    for d in range(1, RUN):
        group_arrived(run_peer, d, run_recv.at[d], run_s, run_r)
        total = total + run_recv[d].astype(F32)
    far_send[...] = total.astype(BF16)
    for d in range(1, far_count):
        to_group(far_peer, d, far_send, far_recv.at[d], far_s, far_r)
    send_eighth(6)
    pass_eighth(2)
    pass_eighth(3)
    send_eighth(7)

    bas_out[...] = bas_send[...]
    for f, (a, b) in enumerate(FACES):
        arrived(a, b, stat_recv.at[f], stat_s.at[f], stat_r.at[f])
        arrived(a, b, bas_recv.at[f], bas_s.at[f], bas_r.at[f])
        basr_out[f] = bas_recv[f]
        lane = lax.broadcasted_iota(jnp.int32, (1, face), 1)
        live = lane < sizes[0, f]
        own = stiff32[:, f * face:(f + 1) * face]
        other = stat_recv[f, primal:primal + 16, :].astype(F32)[:1]
        scale = jnp.where(live, 1.0 / (own + other), 0.0)
        for j in range(face // 128):
            square = jnp.broadcast_to(scale[:, j * 128:(j + 1) * 128], (128, 128))
            dencol[pl.ds(f * face + j * 128, 128), :] = square.T
        own_phi = (stat_send[f, :primal, :].astype(F32) * (own * scale)).astype(BF16)
        other_phi = (stat_recv[f, :primal, :].astype(F32) * (other * scale)).astype(BF16)
        phit[pl.ds(f * face, face), :2 * primal] = jnp.concatenate([own_phi, other_phi], axis=0).T

    for a, b in OFFSETS:
        arrived(a, b, coarse_ext.at[slot_of(a, b)], coarse_s.at[0], coarse_r.at[slot_of(a, b)])
    ext = coarse_ext[...].reshape(9 * cdev, width)
    low_send[...] = dot(sel_t16, ext, ((0,), (0,))).astype(BF16)
    for f, (a, b) in enumerate(FACES):
        beside(a, b, low_send, low_recv.at[f ^ 1], low_s.at[f], low_r.at[f ^ 1])
    total = far_send[...].astype(F32)
    for d in range(1, far_count):
        group_arrived(far_peer, d, far_recv.at[d], far_s, far_r)
        total = total + far_recv[d].astype(F32)
    piece_send[...] = total.astype(BF16)
    for d in range(1, gy_count):
        to_group(gy_peer, d, piece_send, top.at[y], top_s, top_r)
    top[y] = total.astype(BF16)

    low_out[...] = low_send[...]

    for q in range(4):
        part = pl.ds(q * quarter, quarter)
        for f, (a, b) in enumerate(FACES):
            for e in (2 * q, 2 * q + 1):
                rows_e = pl.ds(e * eighth, eighth)
                arrived(a, b, bulk_recv.at[f, rows_e], bulk_s.at[4 * e + f], bulk_r.at[4 * e + f])
            summed = bulk_send[f, part, :].astype(F32) + bulk_recv[f, part, :].astype(F32)
            acc[quarter_rows(f, q), :] = summed * across(dencol[quarter_rows(f, q), :])
    for done in pending:
        done()
    for f, (a, b) in enumerate(FACES):
        arrived(a, b, low_recv.at[f], low_s.at[f], low_r.at[f])
        lowr_out[f] = low_recv[f]
    for d in range(1, gy_count):
        group_arrived(gy_peer, d, top.at[0], top_s, top_r)
    top_out[...] = top[...].astype(F32).reshape(top_size, width)


def finish_kernel(acc, phit, low, lowr, bas, basr, top, out_h, out, sem):
    top_size = top.shape[0]
    primal = low.shape[0]
    face = acc.shape[0] // 4
    top16 = top[...].astype(BF16)

    def full(value, basis):
        return (value.astype(F32) + dot(basis[:, :top_size], top16)).astype(BF16)

    own = full(low[...], bas[...])
    copies = []
    for f in range(4):
        both = jnp.concatenate([own, full(lowr[f], basr[f])], axis=0)
        here = pl.ds(f * face, face)
        out[here, :] = (acc[here, :] + dot(phit[here, :2 * primal], both)).astype(BF16)
        copy = pltpu.make_async_copy(out.at[here], out_h.at[here], sem.at[f])
        copy.start()
        copies.append(copy)
    for copy in copies:
        copy.wait()


def local(gx_count, gy_count, residual, local_inverse, primal_basis, row_stiffness,
          face_sizes, primal_slots, block_inverse, level_basis, top_inverse):
    rows, width = residual.shape[2:]
    face = rows // 4
    primal = primal_basis.shape[2]
    cdev, top_size = level_basis.shape[2:]
    block_size = block_inverse.shape[3]
    far_count = gx_count // RUN
    piece = top_size // gy_count
    vm = pltpu.VMEM
    dma = pltpu.SemaphoreType.DMA
    args = (residual[0, 0], local_inverse[0, 0], primal_basis[0, 0], row_stiffness[0],
            face_sizes[0], primal_slots[0], block_inverse[0, 0], level_basis[0, 0], top_inverse)
    args = [pltpu.with_memory_space_constraint(arg, pltpu.MemorySpace.HBM) for arg in args]
    halo = dma((9,))
    four = dma((4,))
    gys = dma((gy_count,))
    scratch = [
        vm((rows, width), BF16), vm((rows, rows), BF16), vm((primal, rows), BF16),
        vm((1, rows), BF16), pltpu.SMEM((1, 4), jnp.int32), vm((1, primal), jnp.int32),
        vm((cdev, block_size), F32), vm((cdev, top_size), F32), vm((top_size, top_size), F32),
        vm((rows, width), BF16), vm((rows, 128), F32), vm((rows, 128), F32),
        vm((9, cdev, top_size), F32), vm((primal, width), F32),
        vm((9, cdev, width), BF16), vm((9, cdev, width), BF16),
        vm((cdev, width), BF16), vm((block_size, width), BF16), vm((9, cdev, width), BF16),
        vm((4, primal + 16, face), BF16), vm((4, primal + 16, face), BF16),
        vm((4, face, width), BF16), vm((4, face, width), BF16),
        vm((primal, width), BF16), vm((4, primal, width), BF16),
        vm((gy_count, piece, width), BF16), vm((gy_count, piece, width), BF16),
        vm((piece, width), BF16), vm((RUN, piece, width), BF16),
        vm((piece, width), BF16), vm((far_count, piece, width), BF16),
        vm((piece, width), BF16), vm((gy_count, piece, width), BF16),
        vm((primal, 128), BF16), vm((4, primal, 128), BF16),
        vm((4, face // 8, width), BF16), vm((primal + 16, face), BF16),
        dma((11,)), dma((16,)),
        halo, halo, halo, halo, halo, halo,
        four, four, dma((32,)), dma((32,)), four, four, four, four,
        dma((5,)), dma((5,)), gys, gys, gys, gys, dma((RUN,)), dma((RUN,)), dma((far_count,)), dma((far_count,)),
        gys, gys,
    ]
    kept = (
        vm((rows, width), F32), vm((rows, 256), BF16), vm((primal, width), BF16),
        vm((4, primal, width), BF16), vm((primal, 128), BF16), vm((4, primal, 128), BF16),
        vm((top_size, width), F32))
    values = pl.pallas_call(
        functools.partial(apply_kernel, gx_count, gy_count),
        name="apply",
        out_shape=kept,
        in_specs=[pl.BlockSpec(memory_space=pltpu.MemorySpace.HBM)] * len(args),
        out_specs=[pl.BlockSpec(memory_space=pltpu.MemorySpace.VMEM)] * len(kept),
        scratch_shapes=scratch,
        compiler_params=pltpu.CompilerParams(
            collective_id=0, has_side_effects=True, vmem_limit_bytes=40 << 20),
    )(*args)
    out = pl.pallas_call(
        finish_kernel,
        name="finish",
        out_shape=jax.ShapeDtypeStruct((rows, width), BF16),
        in_specs=[pl.BlockSpec(memory_space=pltpu.MemorySpace.VMEM)] * len(kept),
        out_specs=pl.BlockSpec(memory_space=pl.ANY),
        scratch_shapes=[vm((rows, width), BF16), dma((4,))],
        compiler_params=pltpu.CompilerParams(vmem_limit_bytes=16 << 20),
    )(*values)
    return out[None, None]


def solution(mesh):
    in_specs = (
        P("gx", "gy", None, None),
        P("gx", "gy", None, None),
        P("gx", "gy", None, None),
        P("gx", "gy", None),
        P("gx", "gy", None),
        P("gx", "gy", None),
        P("gx", "gy", None, None),
        P("gx", "gy", None, None),
        P(),
    )
    out_specs = P("gx", "gy", None, None)
    body = functools.partial(local, mesh.shape["gx"], mesh.shape["gy"])
    return jax.shard_map(body, mesh=mesh, in_specs=in_specs, out_specs=out_specs, check_vma=False)
```
